32 devices in a mesh: row: 4 (over z), col: 8 (over y, x, core).
Axes of the slice: x: 2, y: 2, z: 4, core: 2. Of those that a mesh axis runs over, the one named last changes fastest.
Arguments:
- fields: bfloat16 [512, 64, 1024], P(None, 'row', 'col'), may hold values from -6 to 6
- enc_mix: bfloat16 [8, 64, 64], replicated, may hold values from -0.5 to 0.5
- k_cycle: bfloat16 [512, 512], P('row', 'col'), may hold values from -0.09375 to 0.09375
- centre_mix: bfloat16 [8, 64, 64], P(None, 'row'), may hold values from -0.4375 to 0.4375
- dec_mix: bfloat16 [8, 64, 64], replicated, may hold values from -0.5 to 0.5
Outputs:
- decoded: bfloat16 [512, 64, 1024], P(None, 'row', 'col')
The draws below stay inside these ranges and needn't reach their ends.
All inputs are finite; a program needn't handle non-finite values.
Results may differ from the reference program's by a relative error of at most 0.014.
Values may be sent and summed in bfloat16 or wider, within the bound.
No kernel may reach another device: no remote copies, remote signals or barrier semaphores. Data moves between devices by JAX's collectives and lax.ppermute only.
A program may use at most 128 MiB of HBM per device.

```python
import math
import jax
import jax.numpy as jnp
import numpy as np
from jax import lax

M = 64
C = 512
NY4 = 64
NX4 = 1024


def levels(own_key, extent, cuts, smallest, top_value):
    level, own = 1.0, jax.random.fold_in(own_key, 6)
    for dim, blocks in cuts:
        heights = jnp.exp(jax.random.uniform(jax.random.fold_in(own, dim), (blocks,), jnp.float32, smallest / len(cuts), top_value / len(cuts)))
        level = level * jnp.repeat(heights, extent[dim] // blocks).reshape([-1 if axis == dim else 1 for axis in range(len(extent))])
    return level


def gaussian(key, shape, deviation, bound, cuts=(), held_as=jnp.bfloat16):
    level = levels(key, shape, cuts, -0.22, 0.18) if cuts else 1.0
    entries = jax.random.normal(key, shape, jnp.float32) * deviation * level
    return jnp.minimum(jnp.maximum(entries, -bound), bound).astype(held_as)


def setup_inputs(seed: int = 0) -> dict:
    splits = jax.random.split(jax.random.key(seed), 6)
    return {
        "fields": gaussian(splits[0], (C, NY4, NX4), 1.0, 6.0, ((1, 4), (2, 8))),
        "enc_mix": gaussian(splits[1], (8, M, M), (2 * M) ** -0.5, 0.5),
        "k_cycle": gaussian(splits[2], (C, C), (9 * C) ** -0.5, 0.09375, ((0, 4), (1, 8))),
        "centre_mix": gaussian(splits[3], (8, M, M), (3 * M) ** -0.5, 0.4375, ((1, 4),)),
        "dec_mix": gaussian(splits[4], (8, M, M), (2 * M) ** -0.5, 0.5),
    }


tap_offsets = ((0, 1), (1, 1), (1, 0), (1, -1), (0, -1), (-1, -1), (-1, 0), (-1, 1))


def rotation_table():
    table = np.zeros((8, 8, 8), np.float32)
    for turn in range(8):
        table[turn, 0, 0] = 1.0
        table[turn, 1, 1] = (-1.0) ** turn
        for frequency in range(1, 4):
            angle_value = 2.0 * math.pi * frequency * turn / 8.0
            first = 2 * frequency
            second = first + 1
            table[turn, first, first] = math.cos(angle_value)
            table[turn, first, second] = -math.sin(angle_value)
            table[turn, second, first] = math.sin(angle_value)
            table[turn, second, second] = math.cos(angle_value)
    return jnp.asarray(table, jnp.float32)


def pattern_table():
    table = np.zeros((8, 8, 8), np.float32)
    table[0, 0, 0] = 1.0
    table[1, 1, 1] = 1.0
    for frequency in range(1, 4):
        first = 2 * frequency
        second = first + 1
        table[first, first, first] = 1.0
        table[first, second, second] = -1.0
        table[second, first, second] = 1.0
        table[second, second, first] = 1.0
    return jnp.asarray(table, jnp.float32)


def irrep_mix(weights, field):
    mults = field.shape[0]
    outputs = [None] * 8
    outputs[0] = jnp.dot(weights[0], field[:, 0], preferred_element_type=jnp.float32)
    outputs[1] = jnp.dot(weights[1], field[:, 1], preferred_element_type=jnp.float32)
    for frequency in range(1, 4):
        first = 2 * frequency
        second = first + 1
        upper = jnp.concatenate([weights[first], -weights[second]], axis=1)
        lower = jnp.concatenate([weights[second], weights[first]], axis=1)
        block = jnp.concatenate([upper, lower], axis=0)
        joined = jnp.concatenate([field[:, first], field[:, second]], axis=0)
        result = jnp.dot(block, joined, preferred_element_type=jnp.float32)
        outputs[first] = result[:mults]
        outputs[second] = result[mults:]
    return jnp.stack(outputs, axis=1)


def gate(values):
    trivial = values[:, 0:1]
    return jnp.concatenate([jax.nn.silu(trivial), values[:, 1:] * jax.nn.sigmoid(trivial)], axis=1)


def cycle_taps(panel, table):
    row_count, col_count = panel.shape
    viewed = panel.astype(jnp.float32).reshape(row_count // 8, 8, col_count // 8, 8)
    turned = jnp.einsum('tab,obic,tdc->toaid', table, viewed, table, precision=lax.Precision.HIGHEST)
    return turned.reshape(8, row_count, col_count).astype(jnp.bfloat16)


def centre_dense(centre):
    outs_m, ins_m = centre.shape[1], centre.shape[2]
    dense = jnp.einsum('abs,soi->oaib', pattern_table(), centre.astype(jnp.float32), precision=lax.Precision.HIGHEST)
    return dense.reshape(outs_m * 8, ins_m * 8).astype(jnp.bfloat16)


def reference(fields, enc_mix, k_cycle, centre_mix, dec_mix):
    chans, height, width = fields.shape
    mults = chans // 8
    blocks = fields.reshape(chans, height // 2, 2, width).transpose(1, 0, 2, 3)

    def encode_rows(block):
        viewed = block.reshape(mults, 8, 2 * width)
        summed = viewed.astype(jnp.float32) + gate(irrep_mix(enc_mix, viewed))
        encoded = summed.astype(jnp.bfloat16).reshape(chans, 2, width)
        pooled = encoded.astype(jnp.float32).reshape(chans, 2, width // 2, 2).mean(axis=(1, 3))
        return encoded, pooled.astype(jnp.bfloat16)

    encoded, pooled = lax.map(encode_rows, blocks)
    ktaps = cycle_taps(k_cycle, rotation_table())
    kcent = centre_dense(centre_mix)
    padded = jnp.pad(pooled, ((1, 1), (0, 0), (0, 0)))
    coarse_rows = pooled.shape[0]

    def conv_row(row_index):
        rows = lax.dynamic_slice_in_dim(padded, row_index, 3, 0)
        total = jnp.dot(kcent, rows[1], preferred_element_type=jnp.float32)
        for tap in range(8):
            shift_y, shift_x = tap_offsets[tap]
            line = jnp.roll(rows[1 + shift_y], -shift_x, axis=1)
            total = total + jnp.dot(ktaps[tap], line, preferred_element_type=jnp.float32)
        gated = gate(total.reshape(mults, 8, -1)).reshape(chans, -1)
        return (rows[1].astype(jnp.float32) + gated).astype(jnp.bfloat16)

    bottleneck = lax.map(conv_row, jnp.arange(coarse_rows, dtype=jnp.int32))

    def decode_rows(pair):
        enc_rows, coarse_line = pair
        upper = jnp.repeat(coarse_line, 2, axis=1)
        merged = (enc_rows.astype(jnp.float32) + upper.astype(jnp.float32)[:, None, :]).astype(jnp.bfloat16)
        viewed = merged.reshape(mults, 8, 2 * width)
        return gate(irrep_mix(dec_mix, viewed)).astype(jnp.bfloat16).reshape(chans, 2, width)

    decoded = lax.map(decode_rows, (encoded, bottleneck))
    return decoded.transpose(1, 0, 2, 3).reshape(chans, height, width)
```

```python
import functools
import math

import jax
import jax.numpy as jnp
import numpy as np
from jax import lax
from jax.experimental import pallas as pl
from jax.experimental.pallas import tpu as pltpu
from jax.sharding import PartitionSpec as P

F32, BF16 = jnp.float32, jnp.bfloat16

COMPONENTS = ((0, 1, 4, 5), (2, 3, 6, 7))
TAPS = ((0, 1), (1, 1), (1, 0), (1, -1))


def place_of(component):
    return (component >> 1) & 1, (component & 1) + 2 * (component >> 2)


def spread_table():
    table = np.zeros((256, 256), np.float32)
    for b in range(4):
        for field in range(64):
            table[b * 64 + field, (field // 8) * 32 + b * 8 + field % 8] = 1.0
    return table


def order_table():
    table = np.zeros((512, 512), np.float32)
    for field in range(64):
        for component in range(8):
            group, b = place_of(component)
            table[field * 8 + component, group * 256 + (field // 8) * 32 + b * 8 + field % 8] = 1.0
    return table


def turn_signs(turn):
    signs = np.zeros((8, 8), np.int64)
    signs[0, 0] = 1
    signs[1, 1] = (-1) ** turn
    for frequency in range(1, 4):
        angle = 2.0 * math.pi * frequency * turn / 8.0
        cosine, sine = np.cos(angle), np.sin(angle)
        block = np.array([[cosine, -sine], [sine, cosine]])
        block[np.abs(block) < 0.1] = 0.0
        first = 2 * frequency
        signs[first : first + 2, first : first + 2] = np.sign(block)
    return signs


def turn_table(turn):
    signs = turn_signs(turn)
    table = np.zeros((2, 256, 256), np.float32)
    for group in range(2):
        for b_from in range(4):
            for b_to in range(4):
                sign = signs[COMPONENTS[group][b_to], COMPONENTS[group][b_from]]
                if sign:
                    for c in range(8):
                        for m in range(8):
                            table[group, c * 32 + b_from * 8 + m, c * 32 + b_to * 8 + m] = sign
    return table


def pool_table():
    table = np.zeros((64, 256), np.float32)
    for x in range(256):
        table[(x % 128) // 2, x] = 0.25
    return table


def dot(a, b):
    return jnp.dot(a, b, preferred_element_type=F32)


def dot_nt(a, b):
    return lax.dot_general(a, b, (((1,), (1,)), ((), ())), preferred_element_type=F32)


def mix_matrix(piece, spread, group):
    parts = [spread[b * 64 : (b + 1) * 64] for b in range(4)]
    if group == 0:
        rows = [dot(piece(0), parts[0]), dot(piece(1), parts[1])]
        u, v = 4, 5
    else:
        rows = [
            dot(piece(2), parts[0]) - dot(piece(3), parts[1]),
            dot(piece(3), parts[0]) + dot(piece(2), parts[1]),
        ]
        u, v = 6, 7
    rows += [
        dot(piece(u), parts[2]) - dot(piece(v), parts[3]),
        dot(piece(v), parts[2]) + dot(piece(u), parts[3]),
    ]
    chunks = [rows[b][c * 8 : (c + 1) * 8] for c in range(8) for b in range(4)]
    return jnp.concatenate(chunks, axis=0).astype(BF16)


def row_start(c, component):
    return ((c * 8) * 8 + component) * 16


def gather_rows(wide, y, group):
    chunks = [
        wide[pl.ds(row_start(c, COMPONENTS[group][b]) + y, 8, stride=128), :]
        for c in range(8)
        for b in range(4)
    ]
    return jnp.concatenate(chunks, axis=0)


def gates(values):
    trivial = values.reshape(8, 4, 8, values.shape[1])[:, 0]
    return jax.nn.sigmoid(trivial)


def gated(values, scale):
    split = values.reshape(8, 4, 8, values.shape[1])
    return (split * scale[:, None]).reshape(values.shape)


def encode_kernel(
    fields, weights, k_local, centre, spread, pool_t,
    encoded, pooled, pay_down, pay_up, pay_own,
    held, wide, sems, *, chunks,
):
    size = 512 // chunks
    copies = []
    for n in range(chunks):
        span = pl.ds(n * size, size)
        copies.append(pltpu.make_async_copy(fields.at[span], held.at[span], sems.at[n]))
        copies[-1].start()
    table = spread[...]
    mixes = [mix_matrix(lambda s: weights[s], table, group) for group in range(2)]
    rows_in, cols_in = k_local.shape
    own_rows = centre.shape[1]
    for j in range(rows_in // 16):
        pay_own[0:16, j * cols_in : (j + 1) * cols_in] = k_local[j * 16 : (j + 1) * 16, :]
    pay_own[16 : 16 + own_rows, :] = jnp.concatenate([centre[s] for s in range(8)], axis=1)
    for n in range(chunks):
        copies[n].wait()
        piece = held[n * size : (n + 1) * size].astype(F32)
        wide[n * size * 16 : (n + 1) * size * 16, :] = piece.reshape(size * 16, 128)

    def step(line, carry):
        result = []
        scale = None
        for group in range(2):
            x = jnp.concatenate(
                [gather_rows(wide, 2 * line, group), gather_rows(wide, 2 * line + 1, group)], axis=1
            )
            y = dot(mixes[group], x.astype(BF16))
            if group == 0:
                scale = gates(y)
            e = (x + gated(y, scale)).astype(BF16)
            encoded[line, group * 256 : (group + 1) * 256, :] = e
            result.append(e)
        mean = dot_nt(pool_t[...], jnp.concatenate(result, axis=0))
        pooled[line] = mean.astype(BF16)
        return carry

    lax.fori_loop(0, 8, step, 0)
    for target, line in ((pay_down, 7), (pay_up, 0)):
        target[0:64, :] = pooled[line]
        target[64:96, :] = pay_own[...]


def middle_kernel(*refs, rows, shape):
    rows_in, cols_in = shape
    pooled, own, above, below = refs[:4]
    others = refs[4 : 4 + rows - 3]
    order = refs[1 + rows]
    near, far, block, raw = refs[2 + rows :]
    row, col = lax.axis_index("row"), lax.axis_index("col")

    def put(source, start, index):
        for j in range(rows_in // 16):
            raw[index, j * 16 : (j + 1) * 16, :] = source[
                start : start + 16, j * cols_in : (j + 1) * cols_in
            ]

    put(own, 0, row)
    put(above, 64, lax.rem(row + rows - 1, rows))
    put(below, 64, lax.rem(row + 1, rows))
    for n, other in enumerate(others):
        put(other, 0, lax.rem(row + rows - 2 - n, rows))
    joined = jnp.concatenate([raw[r] for r in range(rows)], axis=1)
    sorted_block = dot(joined, order[...]).astype(BF16)
    block[...] = sorted_block
    top = above[0:64, :].astype(F32)
    bottom = below[0:64, :].astype(F32)
    top = jnp.where(row > 0, top, 0.0)
    bottom = jnp.where(row < rows - 1, bottom, 0.0)
    lines = [top] + [pooled[line].astype(F32) for line in range(8)] + [bottom]
    blank = jnp.zeros((6, 512), F32)
    left = jnp.concatenate([line[0:1] for line in lines] + [blank], axis=0)
    right = jnp.concatenate([line[63:64] for line in lines] + [blank], axis=0)
    even = lax.rem(col, 2) == 0
    near[0:rows_in, :] = sorted_block
    far[0:rows_in, :] = sorted_block
    near[rows_in : rows_in + 16, :] = jnp.where(even, right, left).astype(BF16)
    far[rows_in : rows_in + 16, :] = jnp.where(even, left, right).astype(BF16)


def pair_steps(cols):
    steps_even = list(range(4, cols, 2))
    steps_odd = steps_even[:-1] + [2]
    return list(zip(steps_even, steps_odd))


def final_kernel(*refs, rows, cols, shape, chunks):
    rows_in, _ = shape
    pairs = pair_steps(cols)
    refs = list(refs)
    pooled, encoded, weights, own, above, below = refs[:6]
    others = refs[6 : 6 + rows - 3]
    refs = refs[6 + rows - 3 :]
    block, near, far = refs[:3]
    near_pairs = refs[3 : 3 + len(pairs)]
    relayed = refs[3 + len(pairs)]
    relayed_pairs = refs[4 + len(pairs) : 4 + 2 * len(pairs)]
    refs = refs[4 + 2 * len(pairs) :]
    spread, turns, decoded = refs[:3]
    kt, turned, padded, left_of, right_of, middle, doubled, centre_rows, wide, out, sems = refs[3:]
    row, col = lax.axis_index("row"), lax.axis_index("col")
    even = lax.rem(col, 2) == 0
    mate = jnp.where(even, col + 1, col - 1)

    for line in range(8):
        padded[line + 1, 8:72, :] = pooled[line].astype(F32)
    padded[0, 8:72, :] = jnp.where(row > 0, above[0:64, :].astype(F32), 0.0)
    padded[9, 8:72, :] = jnp.where(row < rows - 1, below[0:64, :].astype(F32), 0.0)
    near_rim = near[rows_in : rows_in + 16, :].astype(F32)
    far_rim = far[rows_in : rows_in + 16, :].astype(F32)
    left_rim = jnp.where(even, far_rim, near_rim)
    right_rim = jnp.where(even, near_rim, far_rim)
    for line in range(10):
        padded[line, 7:8, :] = left_rim[line : line + 1]
        padded[line, 72:73, :] = right_rim[line : line + 1]

    for line in range(8):
        span = slice(line * 64, line * 64 + 64)
        for tap, (dy, dx) in enumerate(TAPS):
            ahead = padded[line + 1 + dy, 8 + dx : 72 + dx, :]
            behind = padded[line + 1 - dy, 8 - dx : 72 - dx, :]
            plus = (ahead + behind).astype(BF16)
            minus = (ahead - behind).astype(BF16)
            base = tap * 512
            left_of[span, base : base + 256] = plus[:, :256]
            left_of[span, base + 256 : base + 512] = minus[:, 256:]
            right_of[span, base : base + 256] = minus[:, :256]
            right_of[span, base + 256 : base + 512] = plus[:, 256:]

    def put(source, index):
        start = pl.multiple_of(lax.rem(index + 2 * cols, cols) * rows_in, rows_in)
        kt[pl.ds(start, rows_in), :] = source[0:rows_in, :]

    def away(index, step_even, step_odd):
        return index + jnp.where(lax.rem(index, 2) == 0, step_even, step_odd)

    put(block, col)
    put(near, mate)
    put(far, away(col, -1, 1))
    put(relayed, away(mate, -1, 1))
    for n, (step_even, step_odd) in enumerate(pairs):
        put(near_pairs[n], away(col, step_even, step_odd))
        put(relayed_pairs[n], away(mate, step_even, step_odd))

    root = math.sqrt(0.5)
    for tap in range(4):
        signs = turn_signs(tap)
        for group in range(2):
            whole = kt[:, group * 256 : (group + 1) * 256]
            result = whole.astype(F32) if tap == 0 else dot(whole, turns[tap - 1, group])
            turned[0:512, :] = result[:, 0:128]
            turned[512:1024, :] = result[:, 128:256]
            for source in range(2):
                scale = 1.0
                if tap % 2:
                    scale = (1.0, root, 0.5)[group + source]
                comps = COMPONENTS[source]
                for c in range(8):
                    read = {
                        comp: jnp.concatenate(
                            [
                                turned[pl.ds(half * 512 + c * 64 + comp, 8, stride=8), :]
                                for half in range(2)
                            ],
                            axis=1,
                        )
                        for comp in comps
                    }
                    parts = []
                    for comp in comps:
                        total = None
                        for other in comps:
                            sign = int(signs[comp, other])
                            if sign == 0:
                                continue
                            if total is None:
                                total = read[other] if sign > 0 else -read[other]
                            else:
                                total = total + read[other] if sign > 0 else total - read[other]
                        parts.append(total if scale == 1.0 else total * scale)
                    start = tap * 512 + source * 256 + c * 32
                    middle[group, start : start + 32, :] = jnp.concatenate(parts, axis=0).astype(BF16)

    own_rows = 64 // rows
    table = spread[...]

    def put_centre(source, start, index):
        place = pl.multiple_of(index * own_rows, own_rows)
        centre_rows[pl.ds(place, own_rows), :] = source[start : start + own_rows, :].astype(F32)

    put_centre(own, 16, row)
    put_centre(above, 80, lax.rem(row + rows - 1, rows))
    put_centre(below, 80, lax.rem(row + 1, rows))
    for n, other in enumerate(others):
        put_centre(other, 16, lax.rem(row + rows - 2 - n, rows))
    centre = centre_rows[...].astype(BF16)
    centres = [
        mix_matrix(lambda s: centre[:, s * 64 : (s + 1) * 64], table, group) for group in range(2)
    ]
    mixes = [mix_matrix(lambda s: weights[s], table, group) for group in range(2)]

    whole_pooled = jnp.concatenate([pooled[line] for line in range(8)], axis=0)
    totals = [
        dot(side[...], middle[group])
        + dot_nt(whole_pooled[:, group * 256 : (group + 1) * 256], centres[group])
        for group, side in enumerate((left_of, right_of))
    ]
    lane = lax.broadcasted_iota(jnp.int32, (512, 128), 1)
    first = (lane & 31) < 8
    scales = []
    for half in range(2):
        s = jnp.where(first, jax.nn.sigmoid(totals[0][:, half * 128 : half * 128 + 128]), 0.0)
        s = s + pltpu.roll(s, 8, 1)
        scales.append(s + pltpu.roll(s, 16, 1))
    scale = jnp.concatenate(scales + scales, axis=1)
    total = jnp.concatenate(totals, axis=1)
    bottleneck = (whole_pooled.astype(F32) + total * scale).astype(BF16).astype(F32)
    for line in range(8):
        padded[line, 0:64, :] = bottleneck[line * 64 : line * 64 + 64]

    def step(line, carry):
        coarse = padded[line, 0:64, :]
        for quarter in range(4):
            lanes = coarse[:, quarter * 128 : quarter * 128 + 128]
            doubled[pl.ds(quarter * 128, 64, stride=2), :] = lanes
            doubled[pl.ds(quarter * 128 + 1, 64, stride=2), :] = lanes
        fine = jnp.concatenate(
            [doubled[quarter * 128 : quarter * 128 + 128, :] for quarter in range(4)], axis=1
        ).astype(BF16)
        scale = None
        for group in range(2):
            span = slice(group * 256, (group + 1) * 256)
            low = dot_nt(mixes[group], fine[:, span])
            y = dot(mixes[group], encoded[line, span, :]) + jnp.concatenate([low, low], axis=1)
            if group == 0:
                scale = gates(y)
            d = gated(y, scale)
            for half in range(2):
                for c in range(8):
                    for b in range(4):
                        start = row_start(c, COMPONENTS[group][b]) + 2 * line + half
                        at = c * 32 + b * 8
                        wide[pl.ds(start, 8, stride=128), :] = d[
                            at : at + 8, half * 128 : half * 128 + 128
                        ]
        return carry

    lax.fori_loop(0, 8, step, 0)
    size = 512 // chunks
    copies = []
    for n in range(chunks):
        span = pl.ds(n * size, size)
        piece = wide[n * size * 16 : (n + 1) * size * 16, :].astype(BF16)
        out[n * size : (n + 1) * size] = piece.reshape(size, 16, 128)
        copies.append(pltpu.make_async_copy(out.at[span], decoded.at[span], sems.at[n]))
        copies[-1].start()
    for copy in copies:
        copy.wait()


VMEM = pl.BlockSpec(memory_space=pltpu.VMEM)
ANY = pl.BlockSpec(memory_space=pl.ANY)


def params(mebibytes):
    return pltpu.CompilerParams(vmem_limit_bytes=mebibytes * 1024 * 1024)


def per_device(fields, enc_mix, k_cycle, centre_mix, dec_mix):
    rows, cols = lax.axis_size("row"), lax.axis_size("col")
    k_local = k_cycle.T
    shape = k_local.shape
    spread = jnp.asarray(spread_table(), BF16)
    order = jnp.asarray(order_table(), BF16)
    pool_t = jnp.asarray(pool_table(), BF16)
    turns = jnp.asarray(np.stack([turn_table(t) for t in (1, 2, 3)]), BF16)
    arr = lambda *dims: jax.ShapeDtypeStruct(dims, BF16)
    chunks = 4
    encoded, pooled, pay_down, pay_up, pay_own = pl.pallas_call(
        functools.partial(encode_kernel, chunks=chunks),
        out_shape=(arr(8, 512, 256), arr(8, 64, 512), arr(96, 512), arr(96, 512), arr(32, 512)),
        in_specs=[ANY] + [VMEM] * 5,
        out_specs=(VMEM,) * 5,
        scratch_shapes=[
            pltpu.VMEM((512, 16, 128), BF16),
            pltpu.VMEM((8192, 128), F32),
            pltpu.SemaphoreType.DMA((chunks,)),
        ],
        compiler_params=params(40),
        name="encode",
    )(fields, enc_mix, k_local, centre_mix, spread, pool_t)

    def shift(array, step):
        return lax.ppermute(array, "row", [(i, (i + step) % rows) for i in range(rows)])

    above, below = shift(pay_down, 1), shift(pay_up, -1)
    others = [shift(pay_own, step) for step in range(2, rows - 1)]
    near_out, far_out, block = pl.pallas_call(
        functools.partial(middle_kernel, rows=rows, shape=shape),
        out_shape=(arr(shape[0] + 16, 512), arr(shape[0] + 16, 512), arr(shape[0], 512)),
        in_specs=[VMEM] * (2 + rows),
        out_specs=(VMEM,) * 3,
        scratch_shapes=[pltpu.VMEM((rows,) + shape, BF16)],
        compiler_params=params(16),
        name="middle",
    )(pooled, pay_own, above, below, *others, order)

    def mates(array):
        return lax.ppermute(array, "col", [(i, i ^ 1) for i in range(cols)])

    near = mates(near_out)
    far = lax.ppermute(
        far_out, "col", [(i, (i - 1 if i % 2 == 0 else i + 1) % cols) for i in range(cols)]
    )
    near_pairs = [
        lax.ppermute(
            block, "col", [((i + (even, odd)[i % 2]) % cols, i) for i in range(cols)]
        )
        for even, odd in pair_steps(cols)
    ]
    relayed = mates(far)
    relayed_pairs = [mates(array) for array in near_pairs]
    count = 6 + (rows - 3) + 4 + 2 * len(near_pairs) + 2
    return pl.pallas_call(
        functools.partial(final_kernel, rows=rows, cols=cols, shape=shape, chunks=chunks),
        out_shape=jax.ShapeDtypeStruct(fields.shape, BF16),
        in_specs=[VMEM] * count,
        out_specs=ANY,
        scratch_shapes=[
            pltpu.VMEM((512, 512), BF16),
            pltpu.VMEM((1024, 128), F32),
            pltpu.VMEM((10, 80, 512), F32),
            pltpu.VMEM((512, 2048), BF16),
            pltpu.VMEM((512, 2048), BF16),
            pltpu.VMEM((2, 2048, 256), BF16),
            pltpu.VMEM((512, 128), F32),
            pltpu.VMEM((64, 512), F32),
            pltpu.VMEM((8192, 128), F32),
            pltpu.VMEM((512, 16, 128), BF16),
            pltpu.SemaphoreType.DMA((chunks,)),
        ],
        compiler_params=params(48),
        name="final",
    )(
        pooled, encoded, dec_mix, pay_own, above, below, *others,
        block, near, far, *near_pairs, relayed, *relayed_pairs, spread, turns,
    )


def solution(mesh):
    return jax.shard_map(
        per_device,
        mesh=mesh,
        in_specs=(P(None, "row", "col"), P(), P("row", "col"), P(None, "row", None), P()),
        out_specs=P(None, "row", "col"),
        check_vma=False,
    )
```

```python
import functools
import math

import jax
import jax.numpy as jnp
import numpy as np
from jax import lax
from jax.experimental import pallas as pl
from jax.experimental.pallas import tpu as pltpu
from jax.sharding import PartitionSpec as P

F32, BF16 = jnp.float32, jnp.bfloat16

COMPONENTS = ((0, 1, 4, 5), (2, 3, 6, 7))
TAPS = ((0, 1), (1, 1), (1, 0), (1, -1))


def turn_signs(turn):
    signs = np.zeros((8, 8), np.int64)
    signs[0, 0] = 1
    signs[1, 1] = (-1) ** turn
    for frequency in range(1, 4):
        angle = 2.0 * math.pi * frequency * turn / 8.0
        cosine, sine = np.cos(angle), np.sin(angle)
        block = np.array([[cosine, -sine], [sine, cosine]])
        block[np.abs(block) < 0.1] = 0.0
        first = 2 * frequency
        signs[first : first + 2, first : first + 2] = np.sign(block)
    return signs


def turn_table(turn):
    signs = turn_signs(turn)
    table = np.zeros((2, 256, 256), np.float32)
    for group in range(2):
        for b_from in range(4):
            for b_to in range(4):
                sign = signs[COMPONENTS[group][b_to], COMPONENTS[group][b_from]]
                if sign:
                    for c in range(8):
                        for m in range(8):
                            table[group, c * 32 + b_from * 8 + m, c * 32 + b_to * 8 + m] = sign
    return table


def iota(shape, dim):
    return lax.broadcasted_iota(jnp.int32, shape, dim)


def spread_table():
    r, s = iota((256, 256), 0), iota((256, 256), 1)
    target = ((r & 63) >> 3) * 32 + (r >> 6) * 8 + (r & 7)
    return jnp.where(s == target, 1.0, 0.0).astype(BF16)


def order_table():
    r, s = iota((512, 512), 0), iota((512, 512), 1)
    field, component = r >> 3, r & 7
    group, b = (component >> 1) & 1, (component & 1) + 2 * (component >> 2)
    target = group * 256 + (field >> 3) * 32 + b * 8 + (field & 7)
    return jnp.where(s == target, 1.0, 0.0).astype(BF16)


def pool_table():
    x, column = iota((64, 256), 1), iota((64, 256), 0)
    return jnp.where(((x & 127) >> 1) == column, 0.25, 0.0).astype(BF16)


def dot(a, b):
    return jnp.dot(a, b, preferred_element_type=F32)


def dot_nt(a, b):
    return lax.dot_general(a, b, (((1,), (1,)), ((), ())), preferred_element_type=F32)


def mix_matrix(piece, spread, group):
    parts = [spread[b * 64 : (b + 1) * 64] for b in range(4)]
    if group == 0:
        rows = [dot(piece(0), parts[0]), dot(piece(1), parts[1])]
        u, v = 4, 5
    else:
        rows = [
            dot(piece(2), parts[0]) - dot(piece(3), parts[1]),
            dot(piece(3), parts[0]) + dot(piece(2), parts[1]),
        ]
        u, v = 6, 7
    rows += [
        dot(piece(u), parts[2]) - dot(piece(v), parts[3]),
        dot(piece(v), parts[2]) + dot(piece(u), parts[3]),
    ]
    chunks = [rows[b][c * 8 : (c + 1) * 8] for c in range(8) for b in range(4)]
    return jnp.concatenate(chunks, axis=0).astype(BF16)


def row_start(c, component):
    return ((c * 8) * 8 + component) * 16


def gather_rows(wide, y, group):
    chunks = [
        wide[pl.ds(row_start(c, COMPONENTS[group][b]) + y, 8, stride=128), :]
        for c in range(8)
        for b in range(4)
    ]
    return jnp.concatenate(chunks, axis=0)


def gates(values):
    trivial = values.reshape(8, 4, 8, values.shape[1])[:, 0]
    return jax.nn.sigmoid(trivial)


def gated(values, scale):
    split = values.reshape(8, 4, 8, values.shape[1])
    return (split * scale[:, None]).reshape(values.shape)


def encode_line(wide, line, mixes, pool_t):
    result = []
    scale = None
    for group in range(2):
        x = jnp.concatenate(
            [gather_rows(wide, 2 * line, group), gather_rows(wide, 2 * line + 1, group)], axis=1
        )
        y = dot(mixes[group], x.astype(BF16))
        if group == 0:
            scale = gates(y)
        result.append((x + gated(y, scale)).astype(BF16))
    mean = dot_nt(pool_t, jnp.concatenate(result, axis=0))
    return result, mean.astype(BF16)


def edge_kernel(
    fields_in, weights_in, k_in, centre_in,
    wide, encoded, pooled, pay_down, pay_up, pay_own, mixes_out,
    held, weights, k_local, centre, sems, small, *, chunks,
):
    starts = []
    for n, (source, target) in enumerate(
        ((weights_in, weights), (k_in, k_local), (centre_in, centre))
    ):
        starts.append(pltpu.make_async_copy(source, target, small.at[n]))
        starts[-1].start()
    size = 512 // chunks
    copies = []
    for n in range(chunks):
        span = pl.ds(n * size, size)
        copies.append(pltpu.make_async_copy(fields_in.at[span], held.at[span], sems.at[n]))
        copies[-1].start()
    table = spread_table()
    pool_t = pool_table()
    for start in starts:
        start.wait()
    mixes = [mix_matrix(lambda s: weights[s], table, group) for group in range(2)]
    for group in range(2):
        mixes_out[group] = mixes[group]
    rows_in, cols_in = k_local.shape
    own_rows = centre.shape[1]
    for j in range(rows_in // 16):
        pay_own[0:16, j * cols_in : (j + 1) * cols_in] = k_local[j * 16 : (j + 1) * 16, :]
    pay_own[16 : 16 + own_rows, :] = jnp.concatenate([centre[s] for s in range(8)], axis=1)
    for n in range(chunks):
        copies[n].wait()
        piece = held[n * size : (n + 1) * size].astype(F32)
        wide[n * size * 16 : (n + 1) * size * 16, :] = piece.reshape(size * 16, 128)
    for n, (target, line) in enumerate(((pay_up, 0), (pay_down, 7))):
        result, mean = encode_line(wide, line, mixes, pool_t)
        encoded[n, 0:256, :] = result[0]
        encoded[n, 256:512, :] = result[1]
        pooled[n] = mean
        target[0:64, :] = mean
        target[64:96, :] = pay_own[...]


def inner_kernel(wide, edges, mixes_in, weights, pooled, halves, mixes_out):
    table = spread_table()
    pool_t = pool_table()
    mixes = [mixes_in[group] for group in range(2)]
    ends = [mix_matrix(lambda s: weights[s], table, group) for group in range(2)]
    for group in range(2):
        mixes_out[group] = ends[group]

    def step(n, carry):
        result, mean = encode_line(wide, n + 1, mixes, pool_t)
        pooled[n] = mean
        for group in range(2):
            halves[n + 1, group * 256 : (group + 1) * 256, :] = dot(ends[group], result[group])
        return carry

    lax.fori_loop(0, 6, step, 0, unroll=UNROLL)
    for n, line in enumerate((0, 7)):
        for group in range(2):
            span = slice(group * 256, (group + 1) * 256)
            halves[line, span, :] = dot(ends[group], edges[n, span, :])


def rims_kernel(*refs, rows, shape):
    rows_in, cols_in = shape
    ends, inner, own, above, below = refs[:5]
    others = refs[5 : 5 + rows - 3]
    near, far, block, raw = refs[2 + rows :]
    row, col = lax.axis_index("row"), lax.axis_index("col")

    def put(source, start, index):
        for j in range(rows_in // 16):
            raw[index, j * 16 : (j + 1) * 16, :] = source[
                start : start + 16, j * cols_in : (j + 1) * cols_in
            ]

    put(own, 0, row)
    put(above, 64, lax.rem(row + rows - 1, rows))
    put(below, 64, lax.rem(row + 1, rows))
    for n, other in enumerate(others):
        put(other, 0, lax.rem(row + rows - 2 - n, rows))
    joined = jnp.concatenate([raw[r] for r in range(rows)], axis=1)
    sorted_block = dot(joined, order_table()).astype(BF16)
    block[...] = sorted_block
    lines = all_lines(ends, inner, above, below, row, rows)
    blank = jnp.zeros((6, 512), F32)
    left = jnp.concatenate([line[0:1] for line in lines] + [blank], axis=0)
    right = jnp.concatenate([line[63:64] for line in lines] + [blank], axis=0)
    even = lax.rem(col, 2) == 0
    near[0:rows_in, :] = sorted_block
    far[0:rows_in, :] = sorted_block
    near[rows_in : rows_in + 16, :] = jnp.where(even, right, left).astype(BF16)
    far[rows_in : rows_in + 16, :] = jnp.where(even, left, right).astype(BF16)


def own_lines(ends, inner):
    return [ends[0]] + [inner[line] for line in range(6)] + [ends[1]]


def all_lines(ends, inner, above, below, row, rows):
    top = jnp.where(row > 0, above[0:64, :].astype(F32), 0.0)
    bottom = jnp.where(row < rows - 1, below[0:64, :].astype(F32), 0.0)
    return [top] + [line.astype(F32) for line in own_lines(ends, inner)] + [bottom]


def taps_kernel(*refs, rows):
    ends, inner, own, above, below = refs[:5]
    others = refs[5 : 5 + rows - 3]
    left_of, right_of, middle, padded, centre_rows = refs[2 + rows :]
    row = lax.axis_index("row")
    zero = jnp.zeros((1, 512), F32)
    for line, values in enumerate(all_lines(ends, inner, above, below, row, rows)):
        padded[line, 8:72, :] = values
        padded[line, 7:8, :] = zero
        padded[line, 72:73, :] = zero
    for line in range(8):
        span = slice(line * 64, line * 64 + 64)
        for tap, (dy, dx) in enumerate(TAPS):
            ahead = padded[line + 1 + dy, 8 + dx : 72 + dx, :]
            behind = padded[line + 1 - dy, 8 - dx : 72 - dx, :]
            plus = (ahead + behind).astype(BF16)
            minus = (ahead - behind).astype(BF16)
            base = tap * 512
            left_of[span, base : base + 256] = plus[:, :256]
            left_of[span, base + 256 : base + 512] = minus[:, 256:]
            right_of[span, base : base + 256] = minus[:, :256]
            right_of[span, base + 256 : base + 512] = plus[:, 256:]

    own_rows = 64 // rows
    table = spread_table()

    def put_centre(source, start, index):
        place = pl.multiple_of(index * own_rows, own_rows)
        centre_rows[pl.ds(place, own_rows), :] = source[start : start + own_rows, :].astype(F32)

    put_centre(own, 16, row)
    put_centre(above, 80, lax.rem(row + rows - 1, rows))
    put_centre(below, 80, lax.rem(row + 1, rows))
    for n, other in enumerate(others):
        put_centre(other, 16, lax.rem(row + rows - 2 - n, rows))
    centre = centre_rows[...].astype(BF16)
    whole = jnp.concatenate(own_lines(ends, inner), axis=0)
    for group in range(2):
        span = slice(group * 256, (group + 1) * 256)
        matrix = mix_matrix(lambda s: centre[:, s * 64 : (s + 1) * 64], table, group)
        middle[:, span] = dot_nt(whole[:, span], matrix)


def pair_steps(cols):
    steps_even = list(range(4, cols, 2))
    steps_odd = steps_even[:-1] + [2]
    return list(zip(steps_even, steps_odd))


def rim_rows(left_rim, right_rim, group):
    parts = []
    for dy, dx in TAPS:
        if dx == 0:
            parts += [jnp.zeros((16, 512), F32)]
            continue
        first = left_rim[1 - dx * dy : 9 - dx * dy]
        last = right_rim[1 + dx * dy : 9 + dx * dy]
        plus = jnp.concatenate([first, last], axis=0)
        minus = jnp.concatenate([first * float(-dx), last * float(dx)], axis=0)
        pair = (plus, minus) if group == 0 else (minus, plus)
        parts += [pair[0][:, :256], pair[1][:, 256:]]
    return jnp.concatenate(parts, axis=1).astype(BF16)


def final_kernel(*refs, rows, cols, shape, chunks):
    rows_in, _ = shape
    pairs = pair_steps(cols)
    ends, inner, halves, mixes, left_of, right_of, centre = refs[:7]
    block, near, far = refs[7:10]
    near_pairs = refs[10 : 10 + len(pairs)]
    relayed = refs[10 + len(pairs)]
    relayed_pairs = refs[11 + len(pairs) : 11 + 2 * len(pairs)]
    refs = refs[11 + 2 * len(pairs) :]
    turns, decoded = refs[:2]
    kt, turned, middle, coarse, doubled, wide, out, sems = refs[2:]
    col = lax.axis_index("col")
    even = lax.rem(col, 2) == 0
    mate = jnp.where(even, col + 1, col - 1)

    def put(source, index):
        start = pl.multiple_of(lax.rem(index + 2 * cols, cols) * rows_in, rows_in)
        kt[pl.ds(start, rows_in), :] = source[0:rows_in, :]

    def away(index, step_even, step_odd):
        return index + jnp.where(lax.rem(index, 2) == 0, step_even, step_odd)

    put(block, col)
    put(near, mate)
    put(far, away(col, -1, 1))
    put(relayed, away(mate, -1, 1))
    for n, (step_even, step_odd) in enumerate(pairs):
        put(near_pairs[n], away(col, step_even, step_odd))
        put(relayed_pairs[n], away(mate, step_even, step_odd))

    root = math.sqrt(0.5)
    for tap in range(4):
        signs = turn_signs(tap)
        for group in range(2):
            whole = kt[:, group * 256 : (group + 1) * 256]
            result = whole.astype(F32) if tap == 0 else dot(whole, turns[tap - 1, group])
            base = ((tap * 2 + group) % 2) * 1024
            turned[base : base + 512, :] = result[:, 0:128]
            turned[base + 512 : base + 1024, :] = result[:, 128:256]
            for source in range(2):
                scale = 1.0
                if tap % 2:
                    scale = (1.0, root, 0.5)[group + source]
                comps = COMPONENTS[source]
                for c in range(8):
                    read = {
                        comp: jnp.concatenate(
                            [
                                turned[pl.ds(base + half * 512 + c * 64 + comp, 8, stride=8), :]
                                for half in range(2)
                            ],
                            axis=1,
                        )
                        for comp in comps
                    }
                    parts = []
                    for comp in comps:
                        total = None
                        for other in comps:
                            sign = int(signs[comp, other])
                            if sign == 0:
                                continue
                            if total is None:
                                total = read[other] if sign > 0 else -read[other]
                            else:
                                total = total + read[other] if sign > 0 else total - read[other]
                        parts.append(total if scale == 1.0 else total * scale)
                    start = tap * 512 + source * 256 + c * 32
                    middle[group, start : start + 32, :] = jnp.concatenate(parts, axis=0).astype(BF16)

    near_rim = near[rows_in : rows_in + 16, :].astype(F32)
    far_rim = far[rows_in : rows_in + 16, :].astype(F32)
    left_rim = jnp.where(even, far_rim, near_rim)
    right_rim = jnp.where(even, near_rim, far_rim)
    totals = []
    sub = iota((8, 8, 256), 1)
    for group, side in enumerate((left_of, right_of)):
        rows_of = jnp.concatenate([side[...], rim_rows(left_rim, right_rim, group)], axis=0)
        total = dot(rows_of, middle[group])
        extra = total[512:528]
        total = total[0:512] + centre[:, group * 256 : (group + 1) * 256]
        total = total.reshape(8, 8, 8, 256)
        first = total[:, 0] + jnp.where(sub == 0, extra[0:8][:, None, :], 0.0)
        last = total[:, 7] + jnp.where(sub == 7, extra[8:16][:, None, :], 0.0)
        total = jnp.concatenate([first[:, None], total[:, 1:7], last[:, None]], axis=1)
        totals.append(total.reshape(512, 256))
    lane = iota((512, 128), 1)
    is_first = (lane & 31) < 8
    scales = []
    for half in range(2):
        s = jnp.where(is_first, jax.nn.sigmoid(totals[0][:, half * 128 : half * 128 + 128]), 0.0)
        s = s + pltpu.roll(s, 8, 1)
        scales.append(s + pltpu.roll(s, 16, 1))
    scale = jnp.concatenate(scales + scales, axis=1)
    total = jnp.concatenate(totals, axis=1)
    own = jnp.concatenate(own_lines(ends, inner), axis=0).astype(F32)
    coarse[...] = (own + total * scale).astype(BF16).astype(F32).reshape(8, 64, 512)
    matrices = [mixes[group] for group in range(2)]

    def step(line, carry):
        values = coarse[line]
        for quarter in range(4):
            lanes = values[:, quarter * 128 : quarter * 128 + 128]
            doubled[line, pl.ds(quarter * 128, 64, stride=2), :] = lanes
            doubled[line, pl.ds(quarter * 128 + 1, 64, stride=2), :] = lanes
        fine = jnp.concatenate(
            [doubled[line, quarter * 128 : quarter * 128 + 128, :] for quarter in range(4)], axis=1
        ).astype(BF16)
        scale = None
        for group in range(2):
            span = slice(group * 256, (group + 1) * 256)
            low = dot_nt(matrices[group], fine[:, span])
            y = halves[line, span, :] + jnp.concatenate([low, low], axis=1)
            if group == 0:
                scale = gates(y)
            d = gated(y, scale)
            for half in range(2):
                for c in range(8):
                    for b in range(4):
                        start = row_start(c, COMPONENTS[group][b]) + 2 * line + half
                        at = c * 32 + b * 8
                        wide[pl.ds(start, 8, stride=128), :] = d[
                            at : at + 8, half * 128 : half * 128 + 128
                        ]
        return carry

    lax.fori_loop(0, 8, step, 0, unroll=UNROLL)
    size = 512 // chunks
    copies = []
    for n in range(chunks):
        span = pl.ds(n * size, size)
        piece = wide[n * size * 16 : (n + 1) * size * 16, :].astype(BF16)
        out[n * size : (n + 1) * size] = piece.reshape(size, 16, 128)
        copies.append(pltpu.make_async_copy(out.at[span], decoded.at[span], sems.at[n]))
        copies[-1].start()
    for copy in copies:
        copy.wait()


VMEM = pl.BlockSpec(memory_space=pltpu.VMEM)
HBM = pl.BlockSpec(memory_space=pltpu.HBM)
UNROLL = 2


def call(kernel, name, ins, outs, shapes, scratch, mebibytes):
    return pl.pallas_call(
        kernel,
        out_shape=shapes,
        in_specs=ins,
        out_specs=outs,
        scratch_shapes=scratch,
        compiler_params=pltpu.CompilerParams(vmem_limit_bytes=mebibytes * 1024 * 1024),
        name=name,
    )


def arr(*dims, dtype=BF16):
    return jax.ShapeDtypeStruct(dims, dtype)


def per_device(fields, enc_mix, k_cycle, centre_mix, dec_mix):
    rows, cols = lax.axis_size("row"), lax.axis_size("col")
    k_local = k_cycle.T
    shape = k_local.shape
    turns = jnp.asarray(np.stack([turn_table(t) for t in (1, 2, 3)]), BF16)
    chunks = 4
    wide, edges, ends, pay_down, pay_up, pay_own, mixes = call(
        functools.partial(edge_kernel, chunks=chunks),
        "edges",
        [HBM] * 4,
        (VMEM,) * 7,
        (
            arr(8192, 128, dtype=F32), arr(2, 512, 256), arr(2, 64, 512),
            arr(96, 512), arr(96, 512), arr(32, 512), arr(2, 256, 256),
        ),
        [
            pltpu.VMEM((512, 16, 128), BF16),
            pltpu.VMEM(enc_mix.shape, BF16),
            pltpu.VMEM(shape, BF16),
            pltpu.VMEM(centre_mix.shape, BF16),
            pltpu.SemaphoreType.DMA((chunks,)),
            pltpu.SemaphoreType.DMA((3,)),
        ],
        24,
    )(*[pltpu.with_memory_space_constraint(x, pltpu.HBM) for x in (fields, enc_mix, k_local, centre_mix)])

    def shift(array, step):
        return lax.ppermute(array, "row", [(i, (i + step) % rows) for i in range(rows)])

    above, below = shift(pay_down, 1), shift(pay_up, -1)
    others = [shift(pay_own, step) for step in range(2, rows - 1)]
    inner, halves, out_mixes = call(
        inner_kernel,
        "inner",
        [VMEM] * 4,
        (VMEM,) * 3,
        (arr(6, 64, 512), arr(8, 512, 256, dtype=F32), arr(2, 256, 256)),
        [],
        24,
    )(wide, edges, mixes, dec_mix)
    near_out, far_out, block = call(
        functools.partial(rims_kernel, rows=rows, shape=shape),
        "rims",
        [VMEM] * (2 + rows),
        (VMEM,) * 3,
        (arr(shape[0] + 16, 512), arr(shape[0] + 16, 512), arr(shape[0], 512)),
        [pltpu.VMEM((rows,) + shape, BF16)],
        16,
    )(ends, inner, pay_own, above, below, *others)

    def mates(array):
        return lax.ppermute(array, "col", [(i, i ^ 1) for i in range(cols)])

    near = mates(near_out)
    far = lax.ppermute(
        far_out, "col", [(i, (i - 1 if i % 2 == 0 else i + 1) % cols) for i in range(cols)]
    )
    near_pairs = [
        lax.ppermute(
            block, "col", [((i + (even, odd)[i % 2]) % cols, i) for i in range(cols)]
        )
        for even, odd in pair_steps(cols)
    ]
    left_of, right_of, centre = call(
        functools.partial(taps_kernel, rows=rows),
        "taps",
        [VMEM] * (2 + rows),
        (VMEM,) * 3,
        (arr(512, 2048), arr(512, 2048), arr(512, 512, dtype=F32)),
        [pltpu.VMEM((10, 80, 512), F32), pltpu.VMEM((64, 512), F32)],
        24,
    )(ends, inner, pay_own, above, below, *others)
    relayed = mates(far)
    relayed_pairs = [mates(array) for array in near_pairs]
    return call(
        functools.partial(final_kernel, rows=rows, cols=cols, shape=shape, chunks=chunks),
        "final",
        [VMEM] * (12 + 2 * len(near_pairs)),
        HBM,
        jax.ShapeDtypeStruct(fields.shape, BF16),
        [
            pltpu.VMEM((512, 512), BF16),
            pltpu.VMEM((2048, 128), F32),
            pltpu.VMEM((2, 2048, 256), BF16),
            pltpu.VMEM((8, 64, 512), F32),
            pltpu.VMEM((8, 512, 128), F32),
            pltpu.VMEM((8192, 128), F32),
            pltpu.VMEM((512, 16, 128), BF16),
            pltpu.SemaphoreType.DMA((chunks,)),
        ],
        40,
    )(
        ends, inner, halves, out_mixes, left_of, right_of, centre,
        block, near, far, *near_pairs, relayed, *relayed_pairs, turns,
    )


def solution(mesh):
    return jax.shard_map(
        per_device,
        mesh=mesh,
        in_specs=(P(None, "row", "col"), P(), P("row", "col"), P(None, "row", None), P()),
        out_specs=P(None, "row", "col"),
        check_vma=False,
    )
```

```python
import functools
import math

import jax
import jax.numpy as jnp
import numpy as np
from jax import lax
from jax.experimental import pallas as pl
from jax.experimental.pallas import tpu as pltpu
from jax.sharding import PartitionSpec as P

F32, BF16 = jnp.float32, jnp.bfloat16

COMPONENTS = ((0, 1, 4, 5), (2, 3, 6, 7))
TAPS = ((0, 1), (1, 1), (1, 0), (1, -1))


def turn_signs(turn):
    signs = np.zeros((8, 8), np.int64)
    signs[0, 0] = 1
    signs[1, 1] = (-1) ** turn
    for frequency in range(1, 4):
        angle = 2.0 * math.pi * frequency * turn / 8.0
        cosine, sine = np.cos(angle), np.sin(angle)
        block = np.array([[cosine, -sine], [sine, cosine]])
        block[np.abs(block) < 0.1] = 0.0
        first = 2 * frequency
        signs[first : first + 2, first : first + 2] = np.sign(block)
    return signs


def turn_table(turn):
    signs = turn_signs(turn)
    table = np.zeros((2, 256, 256), np.float32)
    for group in range(2):
        for b_from in range(4):
            for b_to in range(4):
                sign = signs[COMPONENTS[group][b_to], COMPONENTS[group][b_from]]
                if sign:
                    for c in range(8):
                        for m in range(8):
                            table[group, c * 32 + b_from * 8 + m, c * 32 + b_to * 8 + m] = sign
    return table


def iota(shape, dim):
    return lax.broadcasted_iota(jnp.int32, shape, dim)


def spread_table():
    r, s = iota((256, 256), 0), iota((256, 256), 1)
    target = ((r & 63) >> 3) * 32 + (r >> 6) * 8 + (r & 7)
    return jnp.where(s == target, 1.0, 0.0).astype(BF16)


def order_table():
    r, s = iota((512, 512), 0), iota((512, 512), 1)
    field, component = r >> 3, r & 7
    group, b = (component >> 1) & 1, (component & 1) + 2 * (component >> 2)
    target = group * 256 + (field >> 3) * 32 + b * 8 + (field & 7)
    return jnp.where(s == target, 1.0, 0.0).astype(BF16)


def pool_table():
    x, column = iota((64, 256), 1), iota((64, 256), 0)
    return jnp.where(((x & 127) >> 1) == column, 0.25, 0.0).astype(BF16)


def dot(a, b):
    return jnp.dot(a, b, preferred_element_type=F32)


def dot_nt(a, b):
    return lax.dot_general(a, b, (((1,), (1,)), ((), ())), preferred_element_type=F32)


def mix_matrix(piece, spread, group):
    parts = [spread[b * 64 : (b + 1) * 64] for b in range(4)]
    if group == 0:
        rows = [dot(piece(0), parts[0]), dot(piece(1), parts[1])]
        u, v = 4, 5
    else:
        rows = [
            dot(piece(2), parts[0]) - dot(piece(3), parts[1]),
            dot(piece(3), parts[0]) + dot(piece(2), parts[1]),
        ]
        u, v = 6, 7
    rows += [
        dot(piece(u), parts[2]) - dot(piece(v), parts[3]),
        dot(piece(v), parts[2]) + dot(piece(u), parts[3]),
    ]
    chunks = [rows[b][c * 8 : (c + 1) * 8] for c in range(8) for b in range(4)]
    return jnp.concatenate(chunks, axis=0).astype(BF16)


def row_start(c, component):
    return c * 8 * PITCH + component * 16


def gather_rows(wide, y, group):
    chunks = [
        wide[pl.ds(row_start(c, COMPONENTS[group][b]) + y, 8, stride=PITCH), :]
        for c in range(8)
        for b in range(4)
    ]
    return jnp.concatenate(chunks, axis=0)


def gates(values):
    trivial = values.reshape(8, 4, 8, values.shape[1])[:, 0]
    return jax.nn.sigmoid(trivial)


def gated(values, scale):
    split = values.reshape(8, 4, 8, values.shape[1])
    return (split * scale[:, None]).reshape(values.shape)


def encode_line(wide, line, mixes, pool_t):
    result = []
    scale = None
    for group in range(2):
        x = jnp.concatenate(
            [gather_rows(wide, 2 * line, group), gather_rows(wide, 2 * line + 1, group)], axis=1
        )
        y = dot(mixes[group], x.astype(BF16))
        if group == 0:
            scale = gates(y)
        result.append((x + gated(y, scale)).astype(BF16))
    mean = dot_nt(pool_t, jnp.concatenate(result, axis=0))
    return result, mean.astype(BF16)


def edge_kernel(
    fields_in, weights_in, k_in, centre_in,
    wide, encoded, pooled, pay_down, pay_up, pay_own, mixes_out,
    held, weights, k_local, centre, sems, small, *, chunks,
):
    starts = []
    for n, (source, target) in enumerate(
        ((weights_in, weights), (k_in, k_local), (centre_in, centre))
    ):
        starts.append(pltpu.make_async_copy(source, target, small.at[n]))
        starts[-1].start()
    size = 512 // chunks
    copies = []
    for n in range(chunks):
        span = pl.ds(n * size, size)
        copies.append(pltpu.make_async_copy(fields_in.at[span], held.at[span], sems.at[n]))
        copies[-1].start()
    table = spread_table()
    pool_t = pool_table()
    for start in starts:
        start.wait()
    mixes = [mix_matrix(lambda s: weights[s], table, group) for group in range(2)]
    for group in range(2):
        mixes_out[group] = mixes[group]
    rows_in, cols_in = k_local.shape
    own_rows = centre.shape[1]
    for j in range(rows_in // 16):
        pay_own[0:16, j * cols_in : (j + 1) * cols_in] = k_local[j * 16 : (j + 1) * 16, :]
    pay_own[16 : 16 + own_rows, :] = jnp.concatenate([centre[s] for s in range(8)], axis=1)
    for n in range(chunks):
        copies[n].wait()
        piece = held[n * size : (n + 1) * size].astype(F32)
        piece = piece.reshape(size * 16, 128)
        for m in range(size // 8):
            at = (n * size // 8 + m) * PITCH
            wide[at : at + 128, :] = piece[m * 128 : m * 128 + 128]
    for n, (target, line) in enumerate(((pay_up, 0), (pay_down, 7))):
        result, mean = encode_line(wide, line, mixes, pool_t)
        encoded[n, 0:256, :] = result[0]
        encoded[n, 256:512, :] = result[1]
        pooled[n] = mean
        target[0:64, :] = mean
        target[64:96, :] = pay_own[...]


def inner_kernel(wide, edges, mixes_in, weights, pooled, halves, mixes_out):
    table = spread_table()
    pool_t = pool_table()
    mixes = [mixes_in[group] for group in range(2)]
    ends = [mix_matrix(lambda s: weights[s], table, group) for group in range(2)]
    for group in range(2):
        mixes_out[group] = ends[group]

    def step(n, carry):
        result, mean = encode_line(wide, n + 1, mixes, pool_t)
        pooled[n] = mean
        for group in range(2):
            halves[n + 1, group * 256 : (group + 1) * 256, :] = dot(ends[group], result[group])
        return carry

    lax.fori_loop(0, 6, step, 0, unroll=UNROLL)
    for n, line in enumerate((0, 7)):
        for group in range(2):
            span = slice(group * 256, (group + 1) * 256)
            halves[line, span, :] = dot(ends[group], edges[n, span, :])


def rims_kernel(*refs, rows, shape):
    rows_in, cols_in = shape
    ends, inner, own, above, below = refs[:5]
    others = refs[5 : 5 + rows - 3]
    near, far, block, raw = refs[2 + rows :]
    row, col = lax.axis_index("row"), lax.axis_index("col")

    def put(source, start, index):
        for j in range(rows_in // 16):
            raw[index, j * 16 : (j + 1) * 16, :] = source[
                start : start + 16, j * cols_in : (j + 1) * cols_in
            ]

    put(own, 0, row)
    put(above, 64, lax.rem(row + rows - 1, rows))
    put(below, 64, lax.rem(row + 1, rows))
    for n, other in enumerate(others):
        put(other, 0, lax.rem(row + rows - 2 - n, rows))
    joined = jnp.concatenate([raw[r] for r in range(rows)], axis=1)
    sorted_block = dot(joined, order_table()).astype(BF16)
    block[...] = sorted_block
    lines = all_lines(ends, inner, above, below, row, rows)
    blank = jnp.zeros((6, 512), F32)
    left = jnp.concatenate([line[0:1] for line in lines] + [blank], axis=0)
    right = jnp.concatenate([line[63:64] for line in lines] + [blank], axis=0)
    even = lax.rem(col, 2) == 0
    near[0:rows_in, :] = sorted_block
    far[0:rows_in, :] = sorted_block
    near[rows_in : rows_in + 16, :] = jnp.where(even, right, left).astype(BF16)
    far[rows_in : rows_in + 16, :] = jnp.where(even, left, right).astype(BF16)


def own_lines(ends, inner):
    return [ends[0]] + [inner[line] for line in range(6)] + [ends[1]]


def all_lines(ends, inner, above, below, row, rows):
    top = jnp.where(row > 0, above[0:64, :].astype(F32), 0.0)
    bottom = jnp.where(row < rows - 1, below[0:64, :].astype(F32), 0.0)
    return [top] + [line.astype(F32) for line in own_lines(ends, inner)] + [bottom]


def taps_kernel(*refs, rows):
    ends, inner, own, above, below = refs[:5]
    others = refs[5 : 5 + rows - 3]
    left_of, right_of, middle, padded, shifted, centre_rows = refs[2 + rows :]
    row = lax.axis_index("row")
    zero = jnp.zeros((1, 512), F32)
    for line, values in enumerate(all_lines(ends, inner, above, below, row, rows)):
        padded[line, 8:72, :] = values
        padded[line, 7:8, :] = zero
        padded[line, 72:73, :] = zero
        shifted[1, line] = values.astype(BF16)
        shifted[0, line] = padded[line, 7:71, :].astype(BF16)
        shifted[2, line] = padded[line, 9:73, :].astype(BF16)
    for line in range(8):
        span = slice(line * 64, line * 64 + 64)
        for tap, (dy, dx) in enumerate(TAPS):
            ahead = shifted[1 + dx, line + 1 + dy]
            behind = shifted[1 - dx, line + 1 - dy]
            plus, minus = ahead + behind, ahead - behind
            base = tap * 512
            left_of[span, base : base + 256] = plus[:, :256]
            left_of[span, base + 256 : base + 512] = minus[:, 256:]
            right_of[span, base : base + 256] = minus[:, :256]
            right_of[span, base + 256 : base + 512] = plus[:, 256:]

    own_rows = 64 // rows
    table = spread_table()

    def put_centre(values, index):
        place = pl.multiple_of(index * own_rows, own_rows)
        centre_rows[pl.ds(place, own_rows), :] = values.astype(F32)

    put_centre(own[16 : 16 + own_rows, :], row)
    put_centre(above[80 : 80 + own_rows, :], lax.rem(row + rows - 1, rows))
    put_centre(below[80 : 80 + own_rows, :], lax.rem(row + 1, rows))
    for n, other in enumerate(others):
        put_centre(other[16 : 16 + own_rows, :], lax.rem(row + rows - 2 - n, rows))
    centre = centre_rows[...].astype(BF16)
    whole = jnp.concatenate(own_lines(ends, inner), axis=0)
    for group in range(2):
        span = slice(group * 256, (group + 1) * 256)
        matrix = mix_matrix(lambda s: centre[:, s * 64 : (s + 1) * 64], table, group)
        middle[:, span] = dot_nt(whole[:, span], matrix)


def pair_steps(cols):
    steps_even = list(range(4, cols, 2))
    steps_odd = steps_even[:-1] + [2]
    return list(zip(steps_even, steps_odd))


def rim_rows(left_rim, right_rim, group):
    parts = []
    for dy, dx in TAPS:
        if dx == 0:
            parts += [jnp.zeros((16, 512), F32)]
            continue
        first = left_rim[1 - dx * dy : 9 - dx * dy]
        last = right_rim[1 + dx * dy : 9 + dx * dy]
        plus = jnp.concatenate([first, last], axis=0)
        minus = jnp.concatenate([first * float(-dx), last * float(dx)], axis=0)
        pair = (plus, minus) if group == 0 else (minus, plus)
        parts += [pair[0][:, :256], pair[1][:, 256:]]
    return jnp.concatenate(parts, axis=1).astype(BF16)


def turn_blocks(blocks, places, turns, turned, middle):
    root = math.sqrt(0.5)
    whole = jnp.concatenate(blocks, axis=0)
    count = whole.shape[0] // 64
    for tap in range(4):
        signs = turn_signs(tap)
        for group in range(2):
            side = whole[:, group * 256 : (group + 1) * 256]
            result = side.astype(F32) if tap == 0 else dot(side, turns[tap - 1, group])
            base = ((tap * 2 + group) % 2) * 1024
            turned[base : base + count * 64, :] = result[:, 0:128]
            turned[base + 512 : base + 512 + count * 64, :] = result[:, 128:256]
            for source in range(2):
                scale = 1.0
                if tap % 2:
                    scale = (1.0, root, 0.5)[group + source]
                comps = COMPONENTS[source]
                for n in range(count):
                    read = {
                        comp: jnp.concatenate(
                            [
                                turned[pl.ds(base + half * 512 + n * 64 + comp, 8, stride=8), :]
                                for half in range(2)
                            ],
                            axis=1,
                        )
                        for comp in comps
                    }
                    parts = []
                    for comp in comps:
                        total = None
                        for other in comps:
                            sign = int(signs[comp, other])
                            if sign == 0:
                                continue
                            if total is None:
                                total = read[other] if sign > 0 else -read[other]
                            else:
                                total = total + read[other] if sign > 0 else total - read[other]
                        parts.append(total if scale == 1.0 else total * scale)
                    start = pl.multiple_of(tap * 512 + source * 256 + places[n] * 32, 32)
                    middle[group, pl.ds(start, 32), :] = jnp.concatenate(parts, axis=0).astype(BF16)


def away(index, step_even, step_odd, cols):
    index = index + jnp.where(lax.rem(index, 2) == 0, step_even, step_odd)
    return lax.rem(index + 2 * cols, cols)


def block_places(col, cols):
    even = lax.rem(col, 2) == 0
    mate = jnp.where(even, col + 1, col - 1)
    steps = [(-1, 1)] + pair_steps(cols)
    first = [col, mate] + [away(col, a, b, cols) for a, b in steps]
    return first, [away(mate, a, b, cols) for a, b in steps]


def early_kernel(*refs, cols, rows_in):
    blocks = refs[: 2 + cols // 2 - 1]
    turns, middle, turned = refs[2 + cols // 2 - 1 :]
    places, _ = block_places(lax.axis_index("col"), cols)
    turn_blocks([block[0:rows_in, :] for block in blocks], places, turns, turned, middle)


def final_kernel(*refs, cols, shape, chunks, split):
    rows_in, _ = shape
    relays = cols // 2 - 1
    ends, inner, halves, mixes, left_of, right_of, centre = refs[:7]
    near, far = refs[7:9]
    refs = refs[9:]
    col = lax.axis_index("col")
    even = lax.rem(col, 2) == 0
    first, second = block_places(col, cols)
    if split:
        relayed, turns = refs[:relays], refs[relays]
        decoded, middle, turned, coarse, doubled, wide, out, sems = refs[relays + 2 :]
        late = [block[0:rows_in, :] for block in relayed]
        places = second
    else:
        held, relayed, turns = refs[: relays], refs[relays : 2 * relays], refs[2 * relays]
        decoded, kt, middle, turned, coarse, doubled, wide, out, sems = refs[2 * relays + 1 :]
        for block, index in zip((held[0], near, far) + held[1:] + relayed, first + second):
            start = pl.multiple_of(index * rows_in, rows_in)
            kt[pl.ds(start, rows_in), :] = block[0:rows_in, :]
        late = [kt[...]]
        places = list(range(8))

    pending = list(late)
    turn_blocks(pending, places, turns, turned, middle)

    near_rim = near[rows_in : rows_in + 16, :].astype(F32)
    far_rim = far[rows_in : rows_in + 16, :].astype(F32)
    left_rim = jnp.where(even, far_rim, near_rim)
    right_rim = jnp.where(even, near_rim, far_rim)
    totals = []
    sub = iota((8, 8, 256), 1)
    for group, side in enumerate((left_of, right_of)):
        rows_of = jnp.concatenate([side[...], rim_rows(left_rim, right_rim, group)], axis=0)
        total = dot(rows_of, middle[group])
        extra = total[512:528]
        total = total[0:512] + centre[:, group * 256 : (group + 1) * 256]
        total = total.reshape(8, 8, 8, 256)
        first = total[:, 0] + jnp.where(sub == 0, extra[0:8][:, None, :], 0.0)
        last = total[:, 7] + jnp.where(sub == 7, extra[8:16][:, None, :], 0.0)
        total = jnp.concatenate([first[:, None], total[:, 1:7], last[:, None]], axis=1)
        totals.append(total.reshape(512, 256))
    lane = iota((512, 128), 1)
    is_first = (lane & 31) < 8
    scales = []
    for half in range(2):
        s = jnp.where(is_first, jax.nn.sigmoid(totals[0][:, half * 128 : half * 128 + 128]), 0.0)
        s = s + pltpu.roll(s, 8, 1)
        scales.append(s + pltpu.roll(s, 16, 1))
    scale = jnp.concatenate(scales + scales, axis=1)
    total = jnp.concatenate(totals, axis=1)
    own = jnp.concatenate(own_lines(ends, inner), axis=0).astype(F32)
    coarse[...] = (own + total * scale).astype(BF16).astype(F32).reshape(8, 64, 512)
    matrices = [mixes[group] for group in range(2)]

    def step(line, carry):
        values = coarse[line]
        for quarter in range(4):
            lanes = values[:, quarter * 128 : quarter * 128 + 128]
            doubled[line, pl.ds(quarter * 128, 64, stride=2), :] = lanes
            doubled[line, pl.ds(quarter * 128 + 1, 64, stride=2), :] = lanes
        fine = jnp.concatenate(
            [doubled[line, quarter * 128 : quarter * 128 + 128, :] for quarter in range(4)], axis=1
        ).astype(BF16)
        scale = None
        for group in range(2):
            span = slice(group * 256, (group + 1) * 256)
            low = dot_nt(matrices[group], fine[:, span])
            y = halves[line, span, :] + jnp.concatenate([low, low], axis=1)
            if group == 0:
                scale = gates(y)
            d = gated(y, scale)
            for half in range(2):
                for c in range(8):
                    for b in range(4):
                        start = row_start(c, COMPONENTS[group][b]) + 2 * line + half
                        at = c * 32 + b * 8
                        wide[pl.ds(start, 8, stride=PITCH), :] = d[
                            at : at + 8, half * 128 : half * 128 + 128
                        ]
        return carry

    lax.fori_loop(0, 8, step, 0, unroll=UNROLL)
    size = 512 // chunks
    copies = []
    for n in range(chunks):
        span = pl.ds(n * size, size)
        for m in range(size // 8):
            at = (n * size // 8 + m) * PITCH
            piece = wide[at : at + 128, :].astype(BF16)
            out[n * size + m * 8 : n * size + m * 8 + 8] = piece.reshape(8, 16, 128)
        copies.append(pltpu.make_async_copy(out.at[span], decoded.at[span], sems.at[n]))
        copies[-1].start()
    for copy in copies:
        copy.wait()


VMEM = pl.BlockSpec(memory_space=pltpu.VMEM)
HBM = pl.BlockSpec(memory_space=pltpu.HBM)
UNROLL = True
PITCH = 136


def call(kernel, name, ins, outs, shapes, scratch, mebibytes, aliases={}):
    return pl.pallas_call(
        kernel,
        out_shape=shapes,
        in_specs=ins,
        out_specs=outs,
        scratch_shapes=scratch,
        compiler_params=pltpu.CompilerParams(vmem_limit_bytes=mebibytes * 1024 * 1024),
        name=name,
        input_output_aliases=aliases,
    )


def arr(*dims, dtype=BF16):
    return jax.ShapeDtypeStruct(dims, dtype)


def per_device(fields, enc_mix, k_cycle, centre_mix, dec_mix):
    rows, cols = lax.axis_size("row"), lax.axis_size("col")
    k_local = k_cycle.T
    shape = k_local.shape

    def shift(array, step):
        return lax.ppermute(array, "row", [(i, (i + step) % rows) for i in range(rows)])

    turns = jnp.asarray(np.stack([turn_table(t) for t in (1, 2, 3)]), BF16)
    chunks = 4
    wide, edges, ends, pay_down, pay_up, pay_own, mixes = call(
        functools.partial(edge_kernel, chunks=chunks),
        "edges",
        [HBM] * 4,
        (VMEM,) * 7,
        (
            arr(64 * PITCH, 128, dtype=F32), arr(2, 512, 256), arr(2, 64, 512),
            arr(96, 512), arr(96, 512), arr(32, 512), arr(2, 256, 256),
        ),
        [
            pltpu.VMEM((512, 16, 128), BF16),
            pltpu.VMEM(enc_mix.shape, BF16),
            pltpu.VMEM(shape, BF16),
            pltpu.VMEM(centre_mix.shape, BF16),
            pltpu.SemaphoreType.DMA((chunks,)),
            pltpu.SemaphoreType.DMA((3,)),
        ],
        24,
    )(*[pltpu.with_memory_space_constraint(x, pltpu.HBM) for x in (fields, enc_mix, k_local, centre_mix)])

    above, below = shift(pay_down, 1), shift(pay_up, -1)
    others = [shift(pay_own, step) for step in range(2, rows - 1)]
    inner, halves, out_mixes = call(
        inner_kernel,
        "inner",
        [VMEM] * 4,
        (VMEM,) * 3,
        (arr(6, 64, 512), arr(8, 512, 256, dtype=F32), arr(2, 256, 256)),
        [],
        24,
    )(wide, edges, mixes, dec_mix)
    near_out, far_out, block = call(
        functools.partial(rims_kernel, rows=rows, shape=shape),
        "rims",
        [VMEM] * (2 + rows),
        (VMEM,) * 3,
        (arr(shape[0] + 16, 512), arr(shape[0] + 16, 512), arr(shape[0], 512)),
        [pltpu.VMEM((rows,) + shape, BF16)],
        16,
    )(ends, inner, pay_own, above, below, *others)

    def mates(array):
        return lax.ppermute(array, "col", [(i, i ^ 1) for i in range(cols)])

    near = mates(near_out)
    far = lax.ppermute(
        far_out, "col", [(i, (i - 1 if i % 2 == 0 else i + 1) % cols) for i in range(cols)]
    )
    near_pairs = [
        lax.ppermute(
            block, "col", [((i + (even, odd)[i % 2]) % cols, i) for i in range(cols)]
        )
        for even, odd in pair_steps(cols)
    ]
    left_of, right_of, centre = call(
        functools.partial(taps_kernel, rows=rows),
        "taps",
        [VMEM] * (2 + rows),
        (VMEM,) * 3,
        (arr(512, 2048), arr(512, 2048), arr(512, 512, dtype=F32)),
        [
            pltpu.VMEM((10, 80, 512), F32),
            pltpu.VMEM((3, 10, 64, 512), BF16),
            pltpu.VMEM((64, 512), F32),
        ],
        24,
    )(ends, inner, pay_own, above, below, *others)
    near, far, near_pairs, left_of, right_of, centre = lax.optimization_barrier(
        (near, far, near_pairs, left_of, right_of, centre)
    )
    relayed = [mates(array) for array in [far] + near_pairs]
    split = shape[0] == 64
    scratch = [
        pltpu.VMEM((2048, 128), F32),
        pltpu.VMEM((8, 64, 512), F32),
        pltpu.VMEM((8, 512, 128), F32),
        pltpu.VMEM((64 * PITCH, 128), F32),
        pltpu.VMEM((512, 16, 128), BF16),
        pltpu.SemaphoreType.DMA((chunks,)),
    ]
    kernel = functools.partial(final_kernel, cols=cols, shape=shape, chunks=chunks, split=split)
    operands = [ends, inner, halves, out_mixes, left_of, right_of, centre, near, far]
    result = jax.ShapeDtypeStruct(fields.shape, BF16)
    if not split:
        operands += [block] + near_pairs + relayed + [turns]
        scratch = [pltpu.VMEM((512, 512), BF16), pltpu.VMEM((2, 2048, 256), BF16)] + scratch
        return call(kernel, "final", [VMEM] * len(operands), HBM, result, scratch, 40)(*operands)
    middle = call(
        functools.partial(early_kernel, cols=cols, rows_in=shape[0]),
        "early",
        [VMEM] * (4 + len(near_pairs)),
        VMEM,
        arr(2, 2048, 256),
        [pltpu.VMEM((2048, 128), F32)],
        24,
    )(block, near, far, *near_pairs, turns)
    operands += relayed + [turns, middle]
    return call(
        kernel, "final", [VMEM] * len(operands), (HBM, VMEM), (result, arr(2, 2048, 256)),
        scratch, 40, aliases={len(operands) - 1: 1},
    )(*operands)[0]


def solution(mesh):
    return jax.shard_map(
        per_device,
        mesh=mesh,
        in_specs=(P(None, "row", "col"), P(), P("row", "col"), P(None, "row", None), P()),
        out_specs=P(None, "row", "col"),
        check_vma=False,
    )
```

```python
import functools
import math

import jax
import jax.numpy as jnp
import numpy as np
from jax import lax
from jax.experimental import pallas as pl
from jax.experimental.pallas import tpu as pltpu
from jax.sharding import PartitionSpec as P

F32, BF16 = jnp.float32, jnp.bfloat16

COMPONENTS = ((0, 1, 4, 5), (2, 3, 6, 7))
TAPS = ((0, 1), (1, 1), (1, 0), (1, -1))


def turn_signs(turn):
    signs = np.zeros((8, 8), np.int64)
    signs[0, 0] = 1
    signs[1, 1] = (-1) ** turn
    for frequency in range(1, 4):
        angle = 2.0 * math.pi * frequency * turn / 8.0
        cosine, sine = np.cos(angle), np.sin(angle)
        block = np.array([[cosine, -sine], [sine, cosine]])
        block[np.abs(block) < 0.1] = 0.0
        first = 2 * frequency
        signs[first : first + 2, first : first + 2] = np.sign(block)
    return signs


def turn_table(turn):
    signs = turn_signs(turn)
    table = np.zeros((2, 256, 256), np.float32)
    for group in range(2):
        for b_from in range(4):
            for b_to in range(4):
                sign = signs[COMPONENTS[group][b_to], COMPONENTS[group][b_from]]
                if sign:
                    for c in range(8):
                        for m in range(8):
                            table[group, c * 32 + b_from * 8 + m, c * 32 + b_to * 8 + m] = sign
    return table


def iota(shape, dim):
    return lax.broadcasted_iota(jnp.int32, shape, dim)


def spread_table():
    r, s = iota((256, 256), 0), iota((256, 256), 1)
    target = ((r & 63) >> 3) * 32 + (r >> 6) * 8 + (r & 7)
    return jnp.where(s == target, 1.0, 0.0).astype(BF16)


def order_table():
    r, s = iota((512, 512), 0), iota((512, 512), 1)
    field, component = r >> 3, r & 7
    group, b = (component >> 1) & 1, (component & 1) + 2 * (component >> 2)
    target = group * 256 + (field >> 3) * 32 + b * 8 + (field & 7)
    return jnp.where(s == target, 1.0, 0.0).astype(BF16)


def pool_table():
    x, column = iota((64, 256), 1), iota((64, 256), 0)
    return jnp.where(((x & 127) >> 1) == column, 0.25, 0.0).astype(BF16)


def dot(a, b):
    return jnp.dot(a, b, preferred_element_type=F32)


def dot_nt(a, b):
    return lax.dot_general(a, b, (((1,), (1,)), ((), ())), preferred_element_type=F32)


def mix_matrix(piece, spread, group):
    parts = [spread[b * 64 : (b + 1) * 64] for b in range(4)]
    if group == 0:
        rows = [dot(piece(0), parts[0]), dot(piece(1), parts[1])]
        u, v = 4, 5
    else:
        rows = [
            dot(piece(2), parts[0]) - dot(piece(3), parts[1]),
            dot(piece(3), parts[0]) + dot(piece(2), parts[1]),
        ]
        u, v = 6, 7
    rows += [
        dot(piece(u), parts[2]) - dot(piece(v), parts[3]),
        dot(piece(v), parts[2]) + dot(piece(u), parts[3]),
    ]
    chunks = [rows[b][c * 8 : (c + 1) * 8] for c in range(8) for b in range(4)]
    return jnp.concatenate(chunks, axis=0).astype(BF16)


def row_start(c, component):
    return c * 8 * PITCH + component * 16


def gather_rows(wide, y, group):
    chunks = [
        wide[pl.ds(row_start(c, COMPONENTS[group][b]) + y, 8, stride=PITCH), :]
        for c in range(8)
        for b in range(4)
    ]
    return jnp.concatenate(chunks, axis=0)


def gates(values):
    trivial = values.reshape(-1, 4, 8, values.shape[1])[:, 0]
    return jax.nn.sigmoid(trivial)


def gated(values, scale):
    split = values.reshape(-1, 4, 8, values.shape[1])
    return (split * scale[:, None]).reshape(values.shape)


def encode_line(wide, line, mixes, pool_t):
    result = []
    scale = None
    for group in range(2):
        x = jnp.concatenate(
            [gather_rows(wide, 2 * line, group), gather_rows(wide, 2 * line + 1, group)], axis=1
        )
        y = dot(mixes[group], x.astype(BF16))
        if group == 0:
            scale = gates(y)
        result.append((x + gated(y, scale)).astype(BF16))
    mean = dot_nt(pool_t, jnp.concatenate(result, axis=0))
    return result, mean.astype(BF16)


def edge_kernel(
    fields_in, weights_in, k_in, centre_in,
    wide, encoded, pooled, pay_down, pay_up, pay_own, mixes_out,
    held, weights, k_local, centre, sems, small, *, chunks,
):
    starts = []
    for n, (source, target) in enumerate(
        ((weights_in, weights), (k_in, k_local), (centre_in, centre))
    ):
        starts.append(pltpu.make_async_copy(source, target, small.at[n]))
        starts[-1].start()
    size = 512 // chunks
    copies = []
    for n in range(chunks):
        span = pl.ds(n * size, size)
        copies.append(pltpu.make_async_copy(fields_in.at[span], held.at[span], sems.at[n]))
        copies[-1].start()
    table = spread_table()
    pool_t = pool_table()
    for start in starts:
        start.wait()
    mixes = [mix_matrix(lambda s: weights[s], table, group) for group in range(2)]
    for group in range(2):
        mixes_out[group] = mixes[group]
    rows_in, cols_in = k_local.shape
    own_rows = centre.shape[1]
    for j in range(rows_in // 16):
        pay_own[0:16, j * cols_in : (j + 1) * cols_in] = k_local[j * 16 : (j + 1) * 16, :]
    first = 4 * lax.rem(lax.axis_index("col"), 2)
    part = jnp.concatenate([centre[first + s].astype(F32) for s in range(4)], axis=1)
    for j in range(own_rows // 8):
        pay_own[16:24, j * 256 : (j + 1) * 256] = part[j * 8 : (j + 1) * 8].astype(BF16)
    for n in range(chunks):
        copies[n].wait()
        piece = held[n * size : (n + 1) * size].astype(F32)
        piece = piece.reshape(size * 16, 128)
        for m in range(size // 8):
            at = (n * size // 8 + m) * PITCH
            wide[at : at + 128, :] = piece[m * 128 : m * 128 + 128]
    for n, (target, line) in enumerate(((pay_up, 0), (pay_down, 7))):
        result, mean = encode_line(wide, line, mixes, pool_t)
        encoded[n, 0:256, :] = result[0]
        encoded[n, 256:512, :] = result[1]
        pooled[n] = mean
        target[0:64, :] = mean
        target[64:88, :] = pay_own[...]


def inner_kernel(wide, edges, mixes_in, weights, pooled, halves, mixes_out):
    table = spread_table()
    pool_t = pool_table()
    mixes = [mixes_in[group] for group in range(2)]
    ends = [mix_matrix(lambda s: weights[s], table, group) for group in range(2)]
    for group in range(2):
        mixes_out[group] = ends[group]

    def step(n, carry):
        result, mean = encode_line(wide, n + 1, mixes, pool_t)
        pooled[n] = mean
        for group in range(2):
            halves[n + 1, group * 256 : (group + 1) * 256, :] = dot(ends[group], result[group])
        return carry

    lax.fori_loop(0, 6, step, 0, unroll=UNROLL)
    for n, line in enumerate((0, 7)):
        for group in range(2):
            span = slice(group * 256, (group + 1) * 256)
            halves[line, span, :] = dot(ends[group], edges[n, span, :])


def rims_kernel(*refs, rows, shape):
    rows_in, cols_in = shape
    ends, inner, own, above, below = refs[:5]
    others = refs[5 : 5 + rows - 3]
    near, far, block, half, raw, parts = refs[2 + rows :]
    row, col = lax.axis_index("row"), lax.axis_index("col")

    own_rows = 64 // rows

    def put(source, start, index):
        for j in range(rows_in // 16):
            raw[index, j * 16 : (j + 1) * 16, :] = source[
                start : start + 16, j * cols_in : (j + 1) * cols_in
            ]
        part = source[start + 16 : start + 24, :].astype(F32)
        for j in range(own_rows // 8):
            place = pl.multiple_of(index * own_rows + j * 8, 8)
            parts[pl.ds(place, 8), :] = part[:, j * 256 : (j + 1) * 256]

    put(own, 0, row)
    put(above, 64, lax.rem(row + rows - 1, rows))
    put(below, 64, lax.rem(row + 1, rows))
    for n, other in enumerate(others):
        put(other, 0, lax.rem(row + rows - 2 - n, rows))
    joined = jnp.concatenate([raw[r] for r in range(rows)], axis=1)
    sorted_block = dot(joined, order_table()).astype(BF16)
    block[...] = sorted_block
    lines = all_lines(ends, inner, above, below, row, rows)
    blank = jnp.zeros((6, 512), F32)
    left = jnp.concatenate([line[0:1] for line in lines] + [blank], axis=0)
    right = jnp.concatenate([line[63:64] for line in lines] + [blank], axis=0)
    even = lax.rem(col, 2) == 0
    near[0:rows_in, :] = sorted_block
    far[0:rows_in, :] = sorted_block
    half[...] = jnp.concatenate([parts[0:32, :], parts[32:64, :]], axis=1).astype(BF16)
    near[rows_in + 16 : rows_in + 48, :] = half[...]
    near[rows_in : rows_in + 16, :] = jnp.where(even, right, left).astype(BF16)
    far[rows_in : rows_in + 16, :] = jnp.where(even, left, right).astype(BF16)


def own_lines(ends, inner):
    return [ends[0]] + [inner[line] for line in range(6)] + [ends[1]]


def all_lines(ends, inner, above, below, row, rows):
    top = jnp.where(row > 0, above[0:64, :].astype(F32), 0.0)
    bottom = jnp.where(row < rows - 1, below[0:64, :].astype(F32), 0.0)
    return [top] + [line.astype(F32) for line in own_lines(ends, inner)] + [bottom]


def taps_kernel(*refs, rows):
    ends, inner, above, below, left_of, right_of, padded, shifted = refs
    row = lax.axis_index("row")
    zero = jnp.zeros((1, 512), F32)
    for line, values in enumerate(all_lines(ends, inner, above, below, row, rows)):
        padded[line, 8:72, :] = values
        padded[line, 7:8, :] = zero
        padded[line, 72:73, :] = zero
        shifted[1, line] = values.astype(BF16)
        shifted[0, line] = padded[line, 7:71, :].astype(BF16)
        shifted[2, line] = padded[line, 9:73, :].astype(BF16)
    for line in range(8):
        span = slice(line * 64, line * 64 + 64)
        for tap, (dy, dx) in enumerate(TAPS):
            ahead = shifted[1 + dx, line + 1 + dy]
            behind = shifted[1 - dx, line + 1 - dy]
            plus, minus = ahead + behind, ahead - behind
            base = tap * 512
            left_of[span, base : base + 256] = plus[:, :256]
            left_of[span, base + 256 : base + 512] = minus[:, 256:]
            right_of[span, base : base + 256] = minus[:, :256]
            right_of[span, base + 256 : base + 512] = plus[:, 256:]


def pair_steps(cols):
    steps_even = list(range(4, cols, 2))
    steps_odd = steps_even[:-1] + [2]
    return list(zip(steps_even, steps_odd))


def rim_rows(left_rim, right_rim, group):
    parts = []
    for dy, dx in TAPS:
        if dx == 0:
            parts += [jnp.zeros((16, 512), F32)]
            continue
        first = left_rim[1 - dx * dy : 9 - dx * dy]
        last = right_rim[1 + dx * dy : 9 + dx * dy]
        plus = jnp.concatenate([first, last], axis=0)
        minus = jnp.concatenate([first * float(-dx), last * float(dx)], axis=0)
        pair = (plus, minus) if group == 0 else (minus, plus)
        parts += [pair[0][:, :256], pair[1][:, 256:]]
    return jnp.concatenate(parts, axis=1).astype(BF16)


def turn_blocks(blocks, places, turns, turned, middle):
    root = math.sqrt(0.5)
    whole = jnp.concatenate(blocks, axis=0)
    count = whole.shape[0] // 64
    for tap in range(4):
        signs = turn_signs(tap)
        for group in range(2):
            side = whole[:, group * 256 : (group + 1) * 256]
            result = side.astype(F32) if tap == 0 else dot(side, turns[tap - 1, group])
            base = ((tap * 2 + group) % 2) * 1024
            turned[base : base + count * 64, :] = result[:, 0:128]
            turned[base + 512 : base + 512 + count * 64, :] = result[:, 128:256]
            for source in range(2):
                scale = 1.0
                if tap % 2:
                    scale = (1.0, root, 0.5)[group + source]
                comps = COMPONENTS[source]
                for n in range(count):
                    read = {
                        comp: jnp.concatenate(
                            [
                                turned[pl.ds(base + half * 512 + n * 64 + comp, 8, stride=8), :]
                                for half in range(2)
                            ],
                            axis=1,
                        )
                        for comp in comps
                    }
                    parts = []
                    for comp in comps:
                        total = None
                        for other in comps:
                            sign = int(signs[comp, other])
                            if sign == 0:
                                continue
                            if total is None:
                                total = read[other] if sign > 0 else -read[other]
                            else:
                                total = total + read[other] if sign > 0 else total - read[other]
                        parts.append(total if scale == 1.0 else total * scale)
                    start = pl.multiple_of(tap * 512 + source * 256 + places[n] * 32, 32)
                    middle[group, pl.ds(start, 32), :] = jnp.concatenate(parts, axis=0).astype(BF16)


def away(index, step_even, step_odd, cols):
    index = index + jnp.where(lax.rem(index, 2) == 0, step_even, step_odd)
    return lax.rem(index + 2 * cols, cols)


def block_places(col, cols):
    even = lax.rem(col, 2) == 0
    mate = jnp.where(even, col + 1, col - 1)
    steps = [(-1, 1)] + pair_steps(cols)
    first = [col, mate] + [away(col, a, b, cols) for a, b in steps]
    return first, [away(mate, a, b, cols) for a, b in steps]


def centre_kernel(ends, inner, half, near, centre, *, rows_in):
    even = lax.rem(lax.axis_index("col"), 2) == 0
    one = half[...].astype(F32)
    two = near[rows_in + 16 : rows_in + 48, :].astype(F32)
    halves = [
        jnp.where(even, one, two).astype(BF16),
        jnp.where(even, two, one).astype(BF16),
    ]

    def piece(s):
        at = (s % 4) * 64
        source = halves[s // 4]
        return jnp.concatenate(
            [source[:, at : at + 64], source[:, 256 + at : 320 + at]], axis=0
        )

    table = spread_table()
    whole = jnp.concatenate(own_lines(ends, inner), axis=0)
    for group in range(2):
        span = slice(group * 256, (group + 1) * 256)
        centre[:, span] = dot_nt(whole[:, span], mix_matrix(piece, table, group))


def early_kernel(*refs, cols, rows_in):
    blocks = refs[: 2 + cols // 2 - 1]
    turns, middle, turned = refs[2 + cols // 2 - 1 :]
    places, _ = block_places(lax.axis_index("col"), cols)
    turn_blocks([block[0:rows_in, :] for block in blocks], places, turns, turned, middle)


def final_kernel(*refs, cols, shape, chunks, split):
    rows_in, _ = shape
    relays = cols // 2 - 1
    ends, inner, halves, mixes, left_of, right_of, centre = refs[:7]
    near, far = refs[7:9]
    refs = refs[9:]
    col = lax.axis_index("col")
    even = lax.rem(col, 2) == 0
    first, second = block_places(col, cols)
    if split:
        relayed, turns = refs[:relays], refs[relays]
        decoded, middle, turned, lows, wide, out, sems = refs[relays + 2 :]
        late = [block[0:rows_in, :] for block in relayed]
        places = second
    else:
        held, relayed, turns = refs[: relays], refs[relays : 2 * relays], refs[2 * relays]
        decoded, kt, middle, turned, lows, wide, out, sems = refs[2 * relays + 1 :]
        for block, index in zip((held[0], near, far) + held[1:] + relayed, first + second):
            start = pl.multiple_of(index * rows_in, rows_in)
            kt[pl.ds(start, rows_in), :] = block[0:rows_in, :]
        late = [kt[...]]
        places = list(range(8))

    pending = list(late)
    turn_blocks(pending, places, turns, turned, middle)

    near_rim = near[rows_in : rows_in + 16, :].astype(F32)
    far_rim = far[rows_in : rows_in + 16, :].astype(F32)
    left_rim = jnp.where(even, far_rim, near_rim)
    right_rim = jnp.where(even, near_rim, far_rim)
    totals = []
    sub = iota((8, 8, 256), 1)
    for group, side in enumerate((left_of, right_of)):
        rows_of = jnp.concatenate([side[...], rim_rows(left_rim, right_rim, group)], axis=0)
        total = dot(rows_of, middle[group])
        extra = total[512:528]
        total = total[0:512] + centre[:, group * 256 : (group + 1) * 256]
        total = total.reshape(8, 8, 8, 256)
        first = total[:, 0] + jnp.where(sub == 0, extra[0:8][:, None, :], 0.0)
        last = total[:, 7] + jnp.where(sub == 7, extra[8:16][:, None, :], 0.0)
        total = jnp.concatenate([first[:, None], total[:, 1:7], last[:, None]], axis=1)
        totals.append(total.reshape(512, 256))
    lane = iota((512, 128), 1)
    is_first = (lane & 31) < 8
    scales = []
    for half in range(2):
        s = jnp.where(is_first, jax.nn.sigmoid(totals[0][:, half * 128 : half * 128 + 128]), 0.0)
        s = s + pltpu.roll(s, 8, 1)
        scales.append(s + pltpu.roll(s, 16, 1))
    scale = jnp.concatenate(scales + scales, axis=1)
    total = jnp.concatenate(totals, axis=1)
    own = jnp.concatenate(own_lines(ends, inner), axis=0).astype(F32)
    bottleneck = (own + total * scale).astype(BF16)
    for group in range(2):
        span = slice(group * 256, (group + 1) * 256)
        for part in range(2):
            lows[part, span, :] = dot_nt(
                mixes[group], bottleneck[part * 256 : (part + 1) * 256, span]
            )
    size = 512 // chunks
    per = 8 // chunks
    copies = []
    for n in range(chunks):
        for line in range(8):
            scale = None
            for group in range(2):
                at = group * 256 + n * per * 32
                index = (iota((per * 32, 128), 1) >> 1) + (line % 2) * 64
                column = ((line % 4) // 2) * 128
                low = lows[line // 4, at : at + per * 32, column : column + 128]
                low = jnp.take_along_axis(low, index, axis=1)
                y = halves[line, at : at + per * 32, :] + jnp.concatenate([low, low], axis=1)
                if group == 0:
                    scale = gates(y)
                d = gated(y, scale)
                for half in range(2):
                    for c in range(per):
                        for b in range(4):
                            start = row_start(n * per + c, COMPONENTS[group][b]) + 2 * line + half
                            at = c * 32 + b * 8
                            wide[pl.ds(start, 8, stride=PITCH), :] = d[
                                at : at + 8, half * 128 : half * 128 + 128
                            ]
        for m in range(size // 8):
            at = (n * size // 8 + m) * PITCH
            piece = wide[at : at + 128, :].astype(BF16)
            out[n * size + m * 8 : n * size + m * 8 + 8] = piece.reshape(8, 16, 128)
        span = pl.ds(n * size, size)
        copies.append(pltpu.make_async_copy(out.at[span], decoded.at[span], sems.at[n]))
        copies[-1].start()
    for copy in copies:
        copy.wait()


VMEM = pl.BlockSpec(memory_space=pltpu.VMEM)
HBM = pl.BlockSpec(memory_space=pltpu.HBM)
UNROLL = True
PITCH = 136


def call(kernel, name, ins, outs, shapes, scratch, mebibytes, aliases={}):
    return pl.pallas_call(
        kernel,
        out_shape=shapes,
        in_specs=ins,
        out_specs=outs,
        scratch_shapes=scratch,
        compiler_params=pltpu.CompilerParams(vmem_limit_bytes=mebibytes * 1024 * 1024),
        name=name,
        input_output_aliases=aliases,
    )


def arr(*dims, dtype=BF16):
    return jax.ShapeDtypeStruct(dims, dtype)


def per_device(fields, enc_mix, k_cycle, centre_mix, dec_mix):
    rows, cols = lax.axis_size("row"), lax.axis_size("col")
    k_local = k_cycle.T
    shape = k_local.shape

    def shift(array, step):
        return lax.ppermute(array, "row", [(i, (i + step) % rows) for i in range(rows)])

    turns = jnp.asarray(np.stack([turn_table(t) for t in (1, 2, 3)]), BF16)
    chunks = 4
    wide, edges, ends, pay_down, pay_up, pay_own, mixes = call(
        functools.partial(edge_kernel, chunks=chunks),
        "edges",
        [HBM] * 4,
        (VMEM,) * 7,
        (
            arr(64 * PITCH, 128, dtype=F32), arr(2, 512, 256), arr(2, 64, 512),
            arr(88, 512), arr(88, 512), arr(24, 512), arr(2, 256, 256),
        ),
        [
            pltpu.VMEM((512, 16, 128), BF16),
            pltpu.VMEM(enc_mix.shape, BF16),
            pltpu.VMEM(shape, BF16),
            pltpu.VMEM(centre_mix.shape, BF16),
            pltpu.SemaphoreType.DMA((chunks,)),
            pltpu.SemaphoreType.DMA((3,)),
        ],
        24,
    )(*[pltpu.with_memory_space_constraint(x, pltpu.HBM) for x in (fields, enc_mix, k_local, centre_mix)])

    above, below = shift(pay_down, 1), shift(pay_up, -1)
    others = [shift(pay_own, step) for step in range(2, rows - 1)]
    inner, halves, out_mixes = call(
        inner_kernel,
        "inner",
        [VMEM] * 4,
        (VMEM,) * 3,
        (arr(6, 64, 512), arr(8, 512, 256, dtype=F32), arr(2, 256, 256)),
        [],
        24,
    )(wide, edges, mixes, dec_mix)
    near_out, far_out, block, half = call(
        functools.partial(rims_kernel, rows=rows, shape=shape),
        "rims",
        [VMEM] * (2 + rows),
        (VMEM,) * 4,
        (arr(shape[0] + 48, 512), arr(shape[0] + 16, 512), arr(shape[0], 512), arr(32, 512)),
        [pltpu.VMEM((rows,) + shape, BF16), pltpu.VMEM((64, 256), F32)],
        16,
    )(ends, inner, pay_own, above, below, *others)

    def mates(array):
        return lax.ppermute(array, "col", [(i, i ^ 1) for i in range(cols)])

    near = mates(near_out)
    far = lax.ppermute(
        far_out, "col", [(i, (i - 1 if i % 2 == 0 else i + 1) % cols) for i in range(cols)]
    )
    near_pairs = [
        lax.ppermute(
            block, "col", [((i + (even, odd)[i % 2]) % cols, i) for i in range(cols)]
        )
        for even, odd in pair_steps(cols)
    ]
    left_of, right_of = call(
        functools.partial(taps_kernel, rows=rows),
        "taps",
        [VMEM] * 4,
        (VMEM,) * 2,
        (arr(512, 2048), arr(512, 2048)),
        [pltpu.VMEM((10, 80, 512), F32), pltpu.VMEM((3, 10, 64, 512), BF16)],
        24,
    )(ends, inner, above, below)
    centre = call(
        functools.partial(centre_kernel, rows_in=shape[0]),
        "centre",
        [VMEM] * 4,
        VMEM,
        arr(512, 512, dtype=F32),
        [],
        16,
    )(ends, inner, half, near)
    near, far, near_pairs, left_of, right_of, centre = lax.optimization_barrier(
        (near, far, near_pairs, left_of, right_of, centre)
    )
    relayed = [mates(array) for array in [far] + near_pairs]
    split = shape[0] == 64
    scratch = [
        pltpu.VMEM((2048, 128), F32),
        pltpu.VMEM((2, 512, 256), F32),
        pltpu.VMEM((64 * PITCH, 128), F32),
        pltpu.VMEM((512, 16, 128), BF16),
        pltpu.SemaphoreType.DMA((chunks,)),
    ]
    kernel = functools.partial(final_kernel, cols=cols, shape=shape, chunks=chunks, split=split)
    operands = [ends, inner, halves, out_mixes, left_of, right_of, centre, near, far]
    result = jax.ShapeDtypeStruct(fields.shape, BF16)
    if not split:
        operands += [block] + near_pairs + relayed + [turns]
        scratch = [pltpu.VMEM((512, 512), BF16), pltpu.VMEM((2, 2048, 256), BF16)] + scratch
        return call(kernel, "final", [VMEM] * len(operands), HBM, result, scratch, 40)(*operands)
    middle = call(
        functools.partial(early_kernel, cols=cols, rows_in=shape[0]),
        "early",
        [VMEM] * (4 + len(near_pairs)),
        VMEM,
        arr(2, 2048, 256),
        [pltpu.VMEM((2048, 128), F32)],
        24,
    )(block, near, far, *near_pairs, turns)
    operands += relayed + [turns, middle]
    return call(
        kernel, "final", [VMEM] * len(operands), (HBM, VMEM), (result, arr(2, 2048, 256)),
        scratch, 40, aliases={len(operands) - 1: 1},
    )(*operands)[0]


def solution(mesh):
    return jax.shard_map(
        per_device,
        mesh=mesh,
        in_specs=(P(None, "row", "col"), P(), P("row", "col"), P(None, "row", None), P()),
        out_specs=P(None, "row", "col"),
        check_vma=False,
    )
```

```python
import functools
import math

import jax
import jax.numpy as jnp
import numpy as np
from jax import lax
from jax.experimental import pallas as pl
from jax.experimental.pallas import tpu as pltpu
from jax.sharding import PartitionSpec as P

F32, BF16 = jnp.float32, jnp.bfloat16

COMPONENTS = ((0, 1, 4, 5), (2, 3, 6, 7))
TAPS = ((0, 1), (1, 1), (1, 0), (1, -1))


def turn_signs(turn):
    signs = np.zeros((8, 8), np.int64)
    signs[0, 0] = 1
    signs[1, 1] = (-1) ** turn
    for frequency in range(1, 4):
        angle = 2.0 * math.pi * frequency * turn / 8.0
        cosine, sine = np.cos(angle), np.sin(angle)
        block = np.array([[cosine, -sine], [sine, cosine]])
        block[np.abs(block) < 0.1] = 0.0
        first = 2 * frequency
        signs[first : first + 2, first : first + 2] = np.sign(block)
    return signs


def turn_table(turn):
    signs = turn_signs(turn)
    table = np.zeros((2, 256, 256), np.float32)
    for group in range(2):
        for b_from in range(4):
            for b_to in range(4):
                sign = signs[COMPONENTS[group][b_to], COMPONENTS[group][b_from]]
                if sign:
                    for c in range(8):
                        for m in range(8):
                            table[group, c * 32 + b_from * 8 + m, c * 32 + b_to * 8 + m] = sign
    return table


def iota(shape, dim):
    return lax.broadcasted_iota(jnp.int32, shape, dim)


def spread_table():
    r, s = iota((256, 256), 0), iota((256, 256), 1)
    target = ((r & 63) >> 3) * 32 + (r >> 6) * 8 + (r & 7)
    return jnp.where(s == target, 1.0, 0.0).astype(BF16)


def order_table():
    r, s = iota((512, 512), 0), iota((512, 512), 1)
    field, component = r >> 3, r & 7
    group, b = (component >> 1) & 1, (component & 1) + 2 * (component >> 2)
    target = group * 256 + (field >> 3) * 32 + b * 8 + (field & 7)
    return jnp.where(s == target, 1.0, 0.0).astype(BF16)


def pool_table():
    x, column = iota((64, 256), 1), iota((64, 256), 0)
    return jnp.where(((x & 127) >> 1) == column, 0.25, 0.0).astype(BF16)


def dot(a, b):
    return jnp.dot(a, b, preferred_element_type=F32)


def dot_nt(a, b):
    return lax.dot_general(a, b, (((1,), (1,)), ((), ())), preferred_element_type=F32)


def mix_matrix(piece, spread, group):
    parts = [spread[b * 64 : (b + 1) * 64] for b in range(4)]
    if group == 0:
        rows = [dot(piece(0), parts[0]), dot(piece(1), parts[1])]
        u, v = 4, 5
    else:
        rows = [
            dot(piece(2), parts[0]) - dot(piece(3), parts[1]),
            dot(piece(3), parts[0]) + dot(piece(2), parts[1]),
        ]
        u, v = 6, 7
    rows += [
        dot(piece(u), parts[2]) - dot(piece(v), parts[3]),
        dot(piece(v), parts[2]) + dot(piece(u), parts[3]),
    ]
    chunks = [rows[b][c * 8 : (c + 1) * 8] for c in range(8) for b in range(4)]
    return jnp.concatenate(chunks, axis=0).astype(BF16)


def row_start(c, component):
    return c * 8 * PITCH + component * 16


def gather_rows(wide, y, group):
    chunks = [
        wide[pl.ds(row_start(c, COMPONENTS[group][b]) + y, 8, stride=PITCH), :]
        for c in range(8)
        for b in range(4)
    ]
    return jnp.concatenate(chunks, axis=0)


def gates(values):
    trivial = values.reshape(-1, 4, 8, values.shape[1])[:, 0]
    return jax.nn.sigmoid(trivial)


def gated(values, scale):
    split = values.reshape(-1, 4, 8, values.shape[1])
    return (split * scale[:, None]).reshape(values.shape)


def encode_line(wide, line, mixes, pool_t):
    result = []
    scale = None
    for group in range(2):
        x = jnp.concatenate(
            [gather_rows(wide, 2 * line, group), gather_rows(wide, 2 * line + 1, group)], axis=1
        )
        y = dot(mixes[group], x.astype(BF16))
        if group == 0:
            scale = gates(y)
        result.append((x + gated(y, scale)).astype(BF16))
    mean = dot_nt(pool_t, jnp.concatenate(result, axis=0))
    return result, mean.astype(BF16)


def edge_kernel(
    fields_in, weights_in, k_in, centre_in,
    wide, encoded, pooled, pay_down, pay_up, pay_own, mixes_out,
    held, weights, k_local, centre, sems, small, *, chunks,
):
    starts = []
    for n, (source, target) in enumerate(
        ((weights_in, weights), (k_in, k_local), (centre_in, centre))
    ):
        starts.append(pltpu.make_async_copy(source, target, small.at[n]))
        starts[-1].start()
    size = 512 // chunks
    copies = []
    for n in range(chunks):
        span = pl.ds(n * size, size)
        copies.append(pltpu.make_async_copy(fields_in.at[span], held.at[span], sems.at[n]))
        copies[-1].start(priority=n % 2)
    table = spread_table()
    pool_t = pool_table()
    for start in starts:
        start.wait()
    mixes = [mix_matrix(lambda s: weights[s], table, group) for group in range(2)]
    for group in range(2):
        mixes_out[group] = mixes[group]
    rows_in, cols_in = k_local.shape
    own_rows = centre.shape[1]
    for j in range(rows_in // 16):
        pay_own[0:16, j * cols_in : (j + 1) * cols_in] = k_local[j * 16 : (j + 1) * 16, :]
    first = 4 * lax.rem(lax.axis_index("col"), 2)
    part = jnp.concatenate([centre[first + s].astype(F32) for s in range(4)], axis=1)
    for j in range(own_rows // 8):
        pay_own[16:24, j * 256 : (j + 1) * 256] = part[j * 8 : (j + 1) * 8].astype(BF16)
    for n in range(chunks):
        copies[n].wait()
        piece = held[n * size : (n + 1) * size].astype(F32)
        piece = piece.reshape(size * 16, 128)
        for m in range(size // 8):
            at = (n * size // 8 + m) * PITCH
            wide[at : at + 128, :] = piece[m * 128 : m * 128 + 128]
    for n, (target, line) in enumerate(((pay_up, 0), (pay_down, 7))):
        result, mean = encode_line(wide, line, mixes, pool_t)
        encoded[n, 0:256, :] = result[0]
        encoded[n, 256:512, :] = result[1]
        pooled[n] = mean
        target[0:64, :] = mean
        target[64:88, :] = pay_own[...]


def inner_kernel(wide, edges, mixes_in, weights, pooled, halves, mixes_out):
    table = spread_table()
    pool_t = pool_table()
    mixes = [mixes_in[group] for group in range(2)]
    ends = [mix_matrix(lambda s: weights[s], table, group) for group in range(2)]
    for group in range(2):
        mixes_out[group] = ends[group]

    def step(n, carry):
        result, mean = encode_line(wide, n + 1, mixes, pool_t)
        pooled[n] = mean
        for group in range(2):
            halves[n + 1, group * 256 : (group + 1) * 256, :] = dot(ends[group], result[group])
        return carry

    lax.fori_loop(0, 6, step, 0, unroll=UNROLL)
    for n, line in enumerate((0, 7)):
        for group in range(2):
            span = slice(group * 256, (group + 1) * 256)
            halves[line, span, :] = dot(ends[group], edges[n, span, :])


def rims_kernel(*refs, rows, shape):
    rows_in, cols_in = shape
    ends, inner, own, above, below = refs[:5]
    others = refs[5 : 5 + rows - 3]
    near, far, block, half, raw, parts = refs[2 + rows :]
    row, col = lax.axis_index("row"), lax.axis_index("col")

    own_rows = 64 // rows

    def put(source, start, index):
        for j in range(rows_in // 16):
            raw[index, j * 16 : (j + 1) * 16, :] = source[
                start : start + 16, j * cols_in : (j + 1) * cols_in
            ]
        part = source[start + 16 : start + 24, :].astype(F32)
        for j in range(own_rows // 8):
            place = pl.multiple_of(index * own_rows + j * 8, 8)
            parts[pl.ds(place, 8), :] = part[:, j * 256 : (j + 1) * 256]

    put(own, 0, row)
    put(above, 64, lax.rem(row + rows - 1, rows))
    put(below, 64, lax.rem(row + 1, rows))
    for n, other in enumerate(others):
        put(other, 0, lax.rem(row + rows - 2 - n, rows))
    joined = jnp.concatenate([raw[r] for r in range(rows)], axis=1)
    sorted_block = dot(joined, order_table()).astype(BF16)
    block[...] = sorted_block
    lines = all_lines(ends, inner, above, below, row, rows)
    blank = jnp.zeros((6, 512), F32)
    left = jnp.concatenate([line[0:1] for line in lines] + [blank], axis=0)
    right = jnp.concatenate([line[63:64] for line in lines] + [blank], axis=0)
    even = lax.rem(col, 2) == 0
    near[0:rows_in, :] = sorted_block
    far[0:rows_in, :] = sorted_block
    half[...] = jnp.concatenate([parts[0:32, :], parts[32:64, :]], axis=1).astype(BF16)
    near[rows_in + 16 : rows_in + 48, :] = half[...]
    near[rows_in : rows_in + 16, :] = jnp.where(even, right, left).astype(BF16)
    far[rows_in : rows_in + 16, :] = jnp.where(even, left, right).astype(BF16)


def own_lines(ends, inner):
    return [ends[0]] + [inner[line] for line in range(6)] + [ends[1]]


def all_lines(ends, inner, above, below, row, rows):
    top = jnp.where(row > 0, above[0:64, :].astype(F32), 0.0)
    bottom = jnp.where(row < rows - 1, below[0:64, :].astype(F32), 0.0)
    return [top] + [line.astype(F32) for line in own_lines(ends, inner)] + [bottom]


def taps_kernel(*refs, rows):
    ends, inner, above, below, left_of, right_of, padded, shifted = refs
    row = lax.axis_index("row")
    zero = jnp.zeros((1, 512), F32)
    for line, values in enumerate(all_lines(ends, inner, above, below, row, rows)):
        padded[line, 8:72, :] = values
        padded[line, 7:8, :] = zero
        padded[line, 72:73, :] = zero
        shifted[1, line] = values.astype(BF16)
        shifted[0, line] = padded[line, 7:71, :].astype(BF16)
        shifted[2, line] = padded[line, 9:73, :].astype(BF16)
    for line in range(8):
        span = slice(line * 64, line * 64 + 64)
        for tap, (dy, dx) in enumerate(TAPS):
            ahead = shifted[1 + dx, line + 1 + dy]
            behind = shifted[1 - dx, line + 1 - dy]
            plus, minus = ahead + behind, ahead - behind
            base = tap * 512
            left_of[span, base : base + 256] = plus[:, :256]
            left_of[span, base + 256 : base + 512] = minus[:, 256:]
            right_of[span, base : base + 256] = minus[:, :256]
            right_of[span, base + 256 : base + 512] = plus[:, 256:]


def pair_steps(cols):
    steps_even = list(range(4, cols, 2))
    steps_odd = steps_even[:-1] + [2]
    return list(zip(steps_even, steps_odd))


def rim_rows(left_rim, right_rim, group):
    parts = []
    for dy, dx in TAPS:
        if dx == 0:
            parts += [jnp.zeros((16, 512), F32)]
            continue
        first = left_rim[1 - dx * dy : 9 - dx * dy]
        last = right_rim[1 + dx * dy : 9 + dx * dy]
        plus = jnp.concatenate([first, last], axis=0)
        minus = jnp.concatenate([first * float(-dx), last * float(dx)], axis=0)
        pair = (plus, minus) if group == 0 else (minus, plus)
        parts += [pair[0][:, :256], pair[1][:, 256:]]
    return jnp.concatenate(parts, axis=1).astype(BF16)


def turn_blocks(blocks, places, turns, turned, middle):
    root = math.sqrt(0.5)
    whole = jnp.concatenate(blocks, axis=0)
    count = whole.shape[0] // 64
    for tap in range(4):
        signs = turn_signs(tap)
        for group in range(2):
            side = whole[:, group * 256 : (group + 1) * 256]
            result = side.astype(F32) if tap == 0 else dot(side, turns[tap - 1, group])
            base = ((tap * 2 + group) % 2) * 1024
            turned[base : base + count * 64, :] = result[:, 0:128]
            turned[base + 512 : base + 512 + count * 64, :] = result[:, 128:256]
            for source in range(2):
                scale = 1.0
                if tap % 2:
                    scale = (1.0, root, 0.5)[group + source]
                comps = COMPONENTS[source]
                for n in range(count):
                    read = {
                        comp: jnp.concatenate(
                            [
                                turned[pl.ds(base + half * 512 + n * 64 + comp, 8, stride=8), :]
                                for half in range(2)
                            ],
                            axis=1,
                        )
                        for comp in comps
                    }
                    parts = []
                    for comp in comps:
                        total = None
                        for other in comps:
                            sign = int(signs[comp, other])
                            if sign == 0:
                                continue
                            if total is None:
                                total = read[other] if sign > 0 else -read[other]
                            else:
                                total = total + read[other] if sign > 0 else total - read[other]
                        parts.append(total if scale == 1.0 else total * scale)
                    start = pl.multiple_of(tap * 512 + source * 256 + places[n] * 32, 32)
                    middle[group, pl.ds(start, 32), :] = jnp.concatenate(parts, axis=0).astype(BF16)


def away(index, step_even, step_odd, cols):
    index = index + jnp.where(lax.rem(index, 2) == 0, step_even, step_odd)
    return lax.rem(index + 2 * cols, cols)


def block_places(col, cols):
    even = lax.rem(col, 2) == 0
    mate = jnp.where(even, col + 1, col - 1)
    steps = [(-1, 1)] + pair_steps(cols)
    first = [col, mate] + [away(col, a, b, cols) for a, b in steps]
    return first, [away(mate, a, b, cols) for a, b in steps]


def centre_kernel(ends, inner, half, near, centre, *, rows_in):
    even = lax.rem(lax.axis_index("col"), 2) == 0
    one = half[...].astype(F32)
    two = near[rows_in + 16 : rows_in + 48, :].astype(F32)
    halves = [
        jnp.where(even, one, two).astype(BF16),
        jnp.where(even, two, one).astype(BF16),
    ]

    def piece(s):
        at = (s % 4) * 64
        source = halves[s // 4]
        return jnp.concatenate(
            [source[:, at : at + 64], source[:, 256 + at : 320 + at]], axis=0
        )

    table = spread_table()
    whole = jnp.concatenate(own_lines(ends, inner), axis=0)
    for group in range(2):
        span = slice(group * 256, (group + 1) * 256)
        centre[:, span] = dot_nt(whole[:, span], mix_matrix(piece, table, group))


def early_kernel(*refs, cols, rows_in):
    blocks = refs[: 2 + cols // 2 - 1]
    turns, middle, turned = refs[2 + cols // 2 - 1 :]
    places, _ = block_places(lax.axis_index("col"), cols)
    turn_blocks([block[0:rows_in, :] for block in blocks], places, turns, turned, middle)


def final_kernel(*refs, cols, shape, chunks, split):
    rows_in, _ = shape
    relays = cols // 2 - 1
    ends, inner, halves, mixes, left_of, right_of, centre = refs[:7]
    near, far = refs[7:9]
    refs = refs[9:]
    col = lax.axis_index("col")
    even = lax.rem(col, 2) == 0
    first, second = block_places(col, cols)
    if split:
        relayed, turns = refs[:relays], refs[relays]
        decoded, middle, turned, lows, wide, out, sems = refs[relays + 2 :]
        late = [block[0:rows_in, :] for block in relayed]
        places = second
    else:
        held, relayed, turns = refs[: relays], refs[relays : 2 * relays], refs[2 * relays]
        decoded, kt, middle, turned, lows, wide, out, sems = refs[2 * relays + 1 :]
        for block, index in zip((held[0], near, far) + held[1:] + relayed, first + second):
            start = pl.multiple_of(index * rows_in, rows_in)
            kt[pl.ds(start, rows_in), :] = block[0:rows_in, :]
        late = [kt[...]]
        places = list(range(8))

    pending = list(late)
    turn_blocks(pending, places, turns, turned, middle)

    near_rim = near[rows_in : rows_in + 16, :].astype(F32)
    far_rim = far[rows_in : rows_in + 16, :].astype(F32)
    left_rim = jnp.where(even, far_rim, near_rim)
    right_rim = jnp.where(even, near_rim, far_rim)
    totals = []
    sub = iota((8, 8, 256), 1)
    for group, side in enumerate((left_of, right_of)):
        rows_of = jnp.concatenate([side[...], rim_rows(left_rim, right_rim, group)], axis=0)
        total = dot(rows_of, middle[group])
        extra = total[512:528]
        total = total[0:512] + centre[:, group * 256 : (group + 1) * 256]
        total = total.reshape(8, 8, 8, 256)
        first = total[:, 0] + jnp.where(sub == 0, extra[0:8][:, None, :], 0.0)
        last = total[:, 7] + jnp.where(sub == 7, extra[8:16][:, None, :], 0.0)
        total = jnp.concatenate([first[:, None], total[:, 1:7], last[:, None]], axis=1)
        totals.append(total.reshape(512, 256))
    lane = iota((512, 128), 1)
    is_first = (lane & 31) < 8
    scales = []
    for half in range(2):
        s = jnp.where(is_first, jax.nn.sigmoid(totals[0][:, half * 128 : half * 128 + 128]), 0.0)
        s = s + pltpu.roll(s, 8, 1)
        scales.append(s + pltpu.roll(s, 16, 1))
    scale = jnp.concatenate(scales + scales, axis=1)
    total = jnp.concatenate(totals, axis=1)
    own = jnp.concatenate(own_lines(ends, inner), axis=0).astype(F32)
    bottleneck = (own + total * scale).astype(BF16)
    for group in range(2):
        span = slice(group * 256, (group + 1) * 256)
        for part in range(2):
            lows[part, span, :] = dot_nt(
                mixes[group], bottleneck[part * 256 : (part + 1) * 256, span]
            )
    size = 512 // chunks
    per = 8 // chunks
    copies = []
    for n in range(chunks):
        for line in range(8):
            scale = None
            for group in range(2):
                at = group * 256 + n * per * 32
                index = (iota((per * 32, 128), 1) >> 1) + (line % 2) * 64
                column = ((line % 4) // 2) * 128
                low = lows[line // 4, at : at + per * 32, column : column + 128]
                low = jnp.take_along_axis(low, index, axis=1)
                y = halves[line, at : at + per * 32, :] + jnp.concatenate([low, low], axis=1)
                if group == 0:
                    scale = gates(y)
                d = gated(y, scale)
                for half in range(2):
                    for c in range(per):
                        for b in range(4):
                            start = row_start(n * per + c, COMPONENTS[group][b]) + 2 * line + half
                            at = c * 32 + b * 8
                            wide[pl.ds(start, 8, stride=PITCH), :] = d[
                                at : at + 8, half * 128 : half * 128 + 128
                            ]
        for m in range(size // 8):
            at = (n * size // 8 + m) * PITCH
            piece = wide[at : at + 128, :].astype(BF16)
            out[n * size + m * 8 : n * size + m * 8 + 8] = piece.reshape(8, 16, 128)
        span = pl.ds(n * size, size)
        copies.append(pltpu.make_async_copy(out.at[span], decoded.at[span], sems.at[n]))
        copies[-1].start()
    for copy in copies:
        copy.wait()


VMEM = pl.BlockSpec(memory_space=pltpu.VMEM)
HBM = pl.BlockSpec(memory_space=pltpu.HBM)
UNROLL = True
PITCH = 136


def call(kernel, name, ins, outs, shapes, scratch, mebibytes, aliases={}):
    return pl.pallas_call(
        kernel,
        out_shape=shapes,
        in_specs=ins,
        out_specs=outs,
        scratch_shapes=scratch,
        compiler_params=pltpu.CompilerParams(vmem_limit_bytes=mebibytes * 1024 * 1024),
        name=name,
        input_output_aliases=aliases,
    )


def arr(*dims, dtype=BF16):
    return jax.ShapeDtypeStruct(dims, dtype)


def per_device(fields, enc_mix, k_cycle, centre_mix, dec_mix):
    rows, cols = lax.axis_size("row"), lax.axis_size("col")
    k_local = k_cycle.T
    shape = k_local.shape

    def shift(array, step):
        return lax.ppermute(array, "row", [(i, (i + step) % rows) for i in range(rows)])

    turns = jnp.asarray(np.stack([turn_table(t) for t in (1, 2, 3)]), BF16)
    chunks = 4
    wide, edges, ends, pay_down, pay_up, pay_own, mixes = call(
        functools.partial(edge_kernel, chunks=chunks),
        "edges",
        [HBM] * 4,
        (VMEM,) * 7,
        (
            arr(64 * PITCH, 128, dtype=F32), arr(2, 512, 256), arr(2, 64, 512),
            arr(88, 512), arr(88, 512), arr(24, 512), arr(2, 256, 256),
        ),
        [
            pltpu.VMEM((512, 16, 128), BF16),
            pltpu.VMEM(enc_mix.shape, BF16),
            pltpu.VMEM(shape, BF16),
            pltpu.VMEM(centre_mix.shape, BF16),
            pltpu.SemaphoreType.DMA((chunks,)),
            pltpu.SemaphoreType.DMA((3,)),
        ],
        24,
    )(*[pltpu.with_memory_space_constraint(x, pltpu.HBM) for x in (fields, enc_mix, k_local, centre_mix)])

    above, below = shift(pay_down, 1), shift(pay_up, -1)
    others = [shift(pay_own, step) for step in range(2, rows - 1)]
    inner, halves, out_mixes = call(
        inner_kernel,
        "inner",
        [VMEM] * 4,
        (VMEM,) * 3,
        (arr(6, 64, 512), arr(8, 512, 256, dtype=F32), arr(2, 256, 256)),
        [],
        24,
    )(wide, edges, mixes, dec_mix)
    near_out, far_out, block, half = call(
        functools.partial(rims_kernel, rows=rows, shape=shape),
        "rims",
        [VMEM] * (2 + rows),
        (VMEM,) * 4,
        (arr(shape[0] + 48, 512), arr(shape[0] + 16, 512), arr(shape[0], 512), arr(32, 512)),
        [pltpu.VMEM((rows,) + shape, BF16), pltpu.VMEM((64, 256), F32)],
        16,
    )(ends, inner, pay_own, above, below, *others)

    def mates(array):
        return lax.ppermute(array, "col", [(i, i ^ 1) for i in range(cols)])

    near = mates(near_out)
    far = lax.ppermute(
        far_out, "col", [(i, (i - 1 if i % 2 == 0 else i + 1) % cols) for i in range(cols)]
    )
    near_pairs = [
        lax.ppermute(
            block, "col", [((i + (even, odd)[i % 2]) % cols, i) for i in range(cols)]
        )
        for even, odd in pair_steps(cols)
    ]
    left_of, right_of = call(
        functools.partial(taps_kernel, rows=rows),
        "taps",
        [VMEM] * 4,
        (VMEM,) * 2,
        (arr(512, 2048), arr(512, 2048)),
        [pltpu.VMEM((10, 80, 512), F32), pltpu.VMEM((3, 10, 64, 512), BF16)],
        24,
    )(ends, inner, above, below)
    centre = call(
        functools.partial(centre_kernel, rows_in=shape[0]),
        "centre",
        [VMEM] * 4,
        VMEM,
        arr(512, 512, dtype=F32),
        [],
        16,
    )(ends, inner, half, near)
    def relay(array):
        return mates(lax.optimization_barrier((array, left_of, right_of, centre))[0])

    relayed = [relay(array) for array in [far] + near_pairs]
    split = shape[0] == 64
    scratch = [
        pltpu.VMEM((2048, 128), F32),
        pltpu.VMEM((2, 512, 256), F32),
        pltpu.VMEM((64 * PITCH, 128), F32),
        pltpu.VMEM((512, 16, 128), BF16),
        pltpu.SemaphoreType.DMA((chunks,)),
    ]
    kernel = functools.partial(final_kernel, cols=cols, shape=shape, chunks=chunks, split=split)
    operands = [ends, inner, halves, out_mixes, left_of, right_of, centre, near, far]
    result = jax.ShapeDtypeStruct(fields.shape, BF16)
    if not split:
        operands += [block] + near_pairs + relayed + [turns]
        scratch = [pltpu.VMEM((512, 512), BF16), pltpu.VMEM((2, 2048, 256), BF16)] + scratch
        return call(kernel, "final", [VMEM] * len(operands), HBM, result, scratch, 40)(*operands)
    middle = call(
        functools.partial(early_kernel, cols=cols, rows_in=shape[0]),
        "early",
        [VMEM] * (4 + len(near_pairs)),
        VMEM,
        arr(2, 2048, 256),
        [pltpu.VMEM((2048, 128), F32)],
        24,
    )(block, near, far, *near_pairs, turns)
    operands += relayed + [turns, middle]
    return call(
        kernel, "final", [VMEM] * len(operands), (HBM, VMEM), (result, arr(2, 2048, 256)),
        scratch, 40, aliases={len(operands) - 1: 1},
    )(*operands)[0]


def solution(mesh):
    return jax.shard_map(
        per_device,
        mesh=mesh,
        in_specs=(P(None, "row", "col"), P(), P("row", "col"), P(None, "row", None), P()),
        out_specs=P(None, "row", "col"),
        check_vma=False,
    )
```

```python
import functools
import math

import jax
import jax.numpy as jnp
import numpy as np
from jax import lax
from jax.experimental import pallas as pl
from jax.experimental.pallas import tpu as pltpu
from jax.sharding import PartitionSpec as P

F32, BF16 = jnp.float32, jnp.bfloat16

COMPONENTS = ((0, 1, 4, 5), (2, 3, 6, 7))
TAPS = ((0, 1), (1, 1), (1, 0), (1, -1))


def turn_signs(turn):
    signs = np.zeros((8, 8), np.int64)
    signs[0, 0] = 1
    signs[1, 1] = (-1) ** turn
    for frequency in range(1, 4):
        angle = 2.0 * math.pi * frequency * turn / 8.0
        cosine, sine = np.cos(angle), np.sin(angle)
        block = np.array([[cosine, -sine], [sine, cosine]])
        block[np.abs(block) < 0.1] = 0.0
        first = 2 * frequency
        signs[first : first + 2, first : first + 2] = np.sign(block)
    return signs


def turn_table(turn):
    signs = turn_signs(turn)
    table = np.zeros((2, 256, 256), np.float32)
    for group in range(2):
        for b_from in range(4):
            for b_to in range(4):
                sign = signs[COMPONENTS[group][b_to], COMPONENTS[group][b_from]]
                if sign:
                    for c in range(8):
                        for m in range(8):
                            table[group, c * 32 + b_from * 8 + m, c * 32 + b_to * 8 + m] = sign
    return table


def iota(shape, dim):
    return lax.broadcasted_iota(jnp.int32, shape, dim)


def spread_table():
    r, s = iota((256, 256), 0), iota((256, 256), 1)
    target = ((r & 63) >> 3) * 32 + (r >> 6) * 8 + (r & 7)
    return jnp.where(s == target, 1.0, 0.0).astype(BF16)


def order_table():
    r, s = iota((512, 512), 0), iota((512, 512), 1)
    field, component = r >> 3, r & 7
    group, b = (component >> 1) & 1, (component & 1) + 2 * (component >> 2)
    target = group * 256 + (field >> 3) * 32 + b * 8 + (field & 7)
    return jnp.where(s == target, 1.0, 0.0).astype(BF16)


def pool_table():
    x, column = iota((64, 256), 1), iota((64, 256), 0)
    return jnp.where(((x & 127) >> 1) == column, 0.25, 0.0).astype(BF16)


def dot(a, b):
    return jnp.dot(a, b, preferred_element_type=F32)


def dot_nt(a, b):
    return lax.dot_general(a, b, (((1,), (1,)), ((), ())), preferred_element_type=F32)


def mix_matrix(piece, spread, group):
    parts = [spread[b * 64 : (b + 1) * 64] for b in range(4)]
    if group == 0:
        rows = [dot(piece(0), parts[0]), dot(piece(1), parts[1])]
        u, v = 4, 5
    else:
        rows = [
            dot(piece(2), parts[0]) - dot(piece(3), parts[1]),
            dot(piece(3), parts[0]) + dot(piece(2), parts[1]),
        ]
        u, v = 6, 7
    rows += [
        dot(piece(u), parts[2]) - dot(piece(v), parts[3]),
        dot(piece(v), parts[2]) + dot(piece(u), parts[3]),
    ]
    chunks = [rows[b][c * 8 : (c + 1) * 8] for c in range(8) for b in range(4)]
    return jnp.concatenate(chunks, axis=0).astype(BF16)


def row_start(c, component):
    return c * 8 * PITCH + component * 16


def gather_rows(wide, y, group):
    chunks = [
        wide[pl.ds(row_start(c, COMPONENTS[group][b]) + y, 8, stride=PITCH), :]
        for c in range(8)
        for b in range(4)
    ]
    return jnp.concatenate(chunks, axis=0)


def gates(values):
    trivial = values.reshape(-1, 4, 8, values.shape[1])[:, 0]
    return jax.nn.sigmoid(trivial)


def gated(values, scale):
    split = values.reshape(-1, 4, 8, values.shape[1])
    return (split * scale[:, None]).reshape(values.shape)


def encode_line(wide, line, mixes, pool_t):
    result = []
    scale = None
    for group in range(2):
        x = jnp.concatenate(
            [gather_rows(wide, 2 * line, group), gather_rows(wide, 2 * line + 1, group)], axis=1
        )
        y = dot(mixes[group], x.astype(BF16))
        if group == 0:
            scale = gates(y)
        result.append((x + gated(y, scale)).astype(BF16))
    mean = dot_nt(pool_t, jnp.concatenate(result, axis=0))
    return result, mean.astype(BF16)


def edge_kernel(
    fields_in, weights_in, k_in, centre_in,
    wide, encoded, pooled, pay_down, pay_up, pay_own, mixes_out,
    held, weights, k_local, centre, sems, small, *, chunks,
):
    starts = []
    for n, (source, target) in enumerate(
        ((weights_in, weights), (k_in, k_local), (centre_in, centre))
    ):
        starts.append(pltpu.make_async_copy(source, target, small.at[n]))
        starts[-1].start()
    size = 512 // chunks
    copies = []
    for n in range(chunks):
        span = pl.ds(n * size, size)
        copies.append(pltpu.make_async_copy(fields_in.at[span], held.at[span], sems.at[n]))
        copies[-1].start(priority=n % 2)
    table = spread_table()
    pool_t = pool_table()
    for start in starts:
        start.wait()
    mixes = [mix_matrix(lambda s: weights[s], table, group) for group in range(2)]
    for group in range(2):
        mixes_out[group] = mixes[group]
    rows_in, cols_in = k_local.shape
    own_rows = centre.shape[1]
    for j in range(rows_in // 16):
        pay_own[0:16, j * cols_in : (j + 1) * cols_in] = k_local[j * 16 : (j + 1) * 16, :]
    first = 4 * lax.rem(lax.axis_index("col"), 2)
    part = jnp.concatenate([centre[first + s].astype(F32) for s in range(4)], axis=1)
    for j in range(own_rows // 8):
        pay_own[16:24, j * 256 : (j + 1) * 256] = part[j * 8 : (j + 1) * 8].astype(BF16)
    for n in range(chunks):
        copies[n].wait()
        piece = held[n * size : (n + 1) * size].astype(F32)
        piece = piece.reshape(size * 16, 128)
        for m in range(size // 8):
            at = (n * size // 8 + m) * PITCH
            wide[at : at + 128, :] = piece[m * 128 : m * 128 + 128]
    for n, (target, line) in enumerate(((pay_up, 0), (pay_down, 7))):
        result, mean = encode_line(wide, line, mixes, pool_t)
        encoded[n, 0:256, :] = result[0]
        encoded[n, 256:512, :] = result[1]
        pooled[n] = mean
        target[0:64, :] = mean
        target[64:88, :] = pay_own[...]


def inner_kernel(wide, edges, mixes_in, weights, pooled, halves, mixes_out, order):
    order[...] = order_table()
    table = spread_table()
    pool_t = pool_table()
    mixes = [mixes_in[group] for group in range(2)]
    ends = [mix_matrix(lambda s: weights[s], table, group) for group in range(2)]
    for group in range(2):
        mixes_out[group] = ends[group]

    def step(n, carry):
        result, mean = encode_line(wide, n + 1, mixes, pool_t)
        pooled[n] = mean
        for group in range(2):
            halves[n + 1, group * 256 : (group + 1) * 256, :] = dot(ends[group], result[group])
        return carry

    lax.fori_loop(0, 6, step, 0, unroll=UNROLL)
    for n, line in enumerate((0, 7)):
        for group in range(2):
            span = slice(group * 256, (group + 1) * 256)
            halves[line, span, :] = dot(ends[group], edges[n, span, :])


def rims_kernel(*refs, rows, shape):
    rows_in, cols_in = shape
    ends, inner, own, above, below = refs[:5]
    others = refs[5 : 5 + rows - 3]
    order = refs[2 + rows]
    near, far, block, half, raw, parts = refs[3 + rows :]
    row, col = lax.axis_index("row"), lax.axis_index("col")

    own_rows = 64 // rows

    def put(source, start, index):
        for j in range(rows_in // 16):
            raw[index, j * 16 : (j + 1) * 16, :] = source[
                start : start + 16, j * cols_in : (j + 1) * cols_in
            ]
        part = source[start + 16 : start + 24, :].astype(F32)
        for j in range(own_rows // 8):
            place = pl.multiple_of(index * own_rows + j * 8, 8)
            parts[pl.ds(place, 8), :] = part[:, j * 256 : (j + 1) * 256]

    put(own, 0, row)
    put(above, 64, lax.rem(row + rows - 1, rows))
    put(below, 64, lax.rem(row + 1, rows))
    for n, other in enumerate(others):
        put(other, 0, lax.rem(row + rows - 2 - n, rows))
    joined = jnp.concatenate([raw[r] for r in range(rows)], axis=1)
    sorted_block = dot(joined, order[...]).astype(BF16)
    block[...] = sorted_block
    lines = all_lines(ends, inner, above, below, row, rows)
    blank = jnp.zeros((6, 512), F32)
    left = jnp.concatenate([line[0:1] for line in lines] + [blank], axis=0)
    right = jnp.concatenate([line[63:64] for line in lines] + [blank], axis=0)
    even = lax.rem(col, 2) == 0
    near[0:rows_in, :] = sorted_block
    far[0:rows_in, :] = sorted_block
    half[...] = jnp.concatenate([parts[0:32, :], parts[32:64, :]], axis=1).astype(BF16)
    near[rows_in + 16 : rows_in + 48, :] = half[...]
    near[rows_in : rows_in + 16, :] = jnp.where(even, right, left).astype(BF16)
    far[rows_in : rows_in + 16, :] = jnp.where(even, left, right).astype(BF16)


def own_lines(ends, inner):
    return [ends[0]] + [inner[line] for line in range(6)] + [ends[1]]


def all_lines(ends, inner, above, below, row, rows):
    top = jnp.where(row > 0, above[0:64, :].astype(F32), 0.0)
    bottom = jnp.where(row < rows - 1, below[0:64, :].astype(F32), 0.0)
    return [top] + [line.astype(F32) for line in own_lines(ends, inner)] + [bottom]


def taps_kernel(*refs, rows):
    ends, inner, above, below, left_of, right_of, padded, shifted = refs
    row = lax.axis_index("row")
    zero = jnp.zeros((1, 512), F32)
    for line, values in enumerate(all_lines(ends, inner, above, below, row, rows)):
        padded[line, 8:72, :] = values
        padded[line, 7:8, :] = zero
        padded[line, 72:73, :] = zero
        shifted[1, line] = values.astype(BF16)
        shifted[0, line] = padded[line, 7:71, :].astype(BF16)
        shifted[2, line] = padded[line, 9:73, :].astype(BF16)
    for line in range(8):
        span = slice(line * 64, line * 64 + 64)
        for tap, (dy, dx) in enumerate(TAPS):
            ahead = shifted[1 + dx, line + 1 + dy]
            behind = shifted[1 - dx, line + 1 - dy]
            plus, minus = ahead + behind, ahead - behind
            base = tap * 512
            left_of[span, base : base + 256] = plus[:, :256]
            left_of[span, base + 256 : base + 512] = minus[:, 256:]
            right_of[span, base : base + 256] = minus[:, :256]
            right_of[span, base + 256 : base + 512] = plus[:, 256:]


def pair_steps(cols):
    steps_even = list(range(4, cols, 2))
    steps_odd = steps_even[:-1] + [2]
    return list(zip(steps_even, steps_odd))


def rim_rows(left_rim, right_rim, group):
    parts = []
    for dy, dx in TAPS:
        if dx == 0:
            parts += [jnp.zeros((16, 512), F32)]
            continue
        first = left_rim[1 - dx * dy : 9 - dx * dy]
        last = right_rim[1 + dx * dy : 9 + dx * dy]
        plus = jnp.concatenate([first, last], axis=0)
        minus = jnp.concatenate([first * float(-dx), last * float(dx)], axis=0)
        pair = (plus, minus) if group == 0 else (minus, plus)
        parts += [pair[0][:, :256], pair[1][:, 256:]]
    return jnp.concatenate(parts, axis=1).astype(BF16)


def turn_blocks(blocks, places, turns, turned, middle):
    root = math.sqrt(0.5)
    whole = jnp.concatenate(blocks, axis=0)
    count = whole.shape[0] // 64
    for tap in range(4):
        signs = turn_signs(tap)
        for group in range(2):
            side = whole[:, group * 256 : (group + 1) * 256]
            result = side.astype(F32) if tap == 0 else dot(side, turns[tap - 1, group])
            base = ((tap * 2 + group) % 2) * 1024
            turned[base : base + count * 64, :] = result[:, 0:128]
            turned[base + 512 : base + 512 + count * 64, :] = result[:, 128:256]
            for source in range(2):
                scale = 1.0
                if tap % 2:
                    scale = (1.0, root, 0.5)[group + source]
                comps = COMPONENTS[source]
                for n in range(count):
                    read = {
                        comp: jnp.concatenate(
                            [
                                turned[pl.ds(base + half * 512 + n * 64 + comp, 8, stride=8), :]
                                for half in range(2)
                            ],
                            axis=1,
                        )
                        for comp in comps
                    }
                    parts = []
                    for comp in comps:
                        total = None
                        for other in comps:
                            sign = int(signs[comp, other])
                            if sign == 0:
                                continue
                            if total is None:
                                total = read[other] if sign > 0 else -read[other]
                            else:
                                total = total + read[other] if sign > 0 else total - read[other]
                        parts.append(total if scale == 1.0 else total * scale)
                    start = pl.multiple_of(tap * 512 + source * 256 + places[n] * 32, 32)
                    middle[group, pl.ds(start, 32), :] = jnp.concatenate(parts, axis=0).astype(BF16)


def away(index, step_even, step_odd, cols):
    index = index + jnp.where(lax.rem(index, 2) == 0, step_even, step_odd)
    return lax.rem(index + 2 * cols, cols)


def block_places(col, cols):
    even = lax.rem(col, 2) == 0
    mate = jnp.where(even, col + 1, col - 1)
    steps = [(-1, 1)] + pair_steps(cols)
    first = [col, mate] + [away(col, a, b, cols) for a, b in steps]
    return first, [away(mate, a, b, cols) for a, b in steps]


def centre_kernel(ends, inner, half, near, centre, *, rows_in):
    even = lax.rem(lax.axis_index("col"), 2) == 0
    one = half[...].astype(F32)
    two = near[rows_in + 16 : rows_in + 48, :].astype(F32)
    halves = [
        jnp.where(even, one, two).astype(BF16),
        jnp.where(even, two, one).astype(BF16),
    ]

    def piece(s):
        at = (s % 4) * 64
        source = halves[s // 4]
        return jnp.concatenate(
            [source[:, at : at + 64], source[:, 256 + at : 320 + at]], axis=0
        )

    table = spread_table()
    whole = jnp.concatenate(own_lines(ends, inner), axis=0)
    for group in range(2):
        span = slice(group * 256, (group + 1) * 256)
        centre[:, span] = dot_nt(whole[:, span], mix_matrix(piece, table, group))


def early_kernel(*refs, cols, rows_in):
    blocks = refs[: 2 + cols // 2 - 1]
    turns, middle, turned = refs[2 + cols // 2 - 1 :]
    places, _ = block_places(lax.axis_index("col"), cols)
    turn_blocks([block[0:rows_in, :] for block in blocks], places, turns, turned, middle)


def final_kernel(*refs, cols, shape, chunks, split):
    rows_in, _ = shape
    relays = cols // 2 - 1
    ends, inner, halves, mixes, left_of, right_of, centre = refs[:7]
    near, far = refs[7:9]
    refs = refs[9:]
    col = lax.axis_index("col")
    even = lax.rem(col, 2) == 0
    first, second = block_places(col, cols)
    if split:
        relayed, turns = refs[:relays], refs[relays]
        decoded, middle, turned, lows, wide, out, sems = refs[relays + 2 :]
        late = [block[0:rows_in, :] for block in relayed]
        places = second
    else:
        held, relayed, turns = refs[: relays], refs[relays : 2 * relays], refs[2 * relays]
        decoded, kt, middle, turned, lows, wide, out, sems = refs[2 * relays + 1 :]
        for block, index in zip((held[0], near, far) + held[1:] + relayed, first + second):
            start = pl.multiple_of(index * rows_in, rows_in)
            kt[pl.ds(start, rows_in), :] = block[0:rows_in, :]
        late = [kt[...]]
        places = list(range(8))

    pending = list(late)
    turn_blocks(pending, places, turns, turned, middle)

    near_rim = near[rows_in : rows_in + 16, :].astype(F32)
    far_rim = far[rows_in : rows_in + 16, :].astype(F32)
    left_rim = jnp.where(even, far_rim, near_rim)
    right_rim = jnp.where(even, near_rim, far_rim)
    totals = []
    sub = iota((8, 8, 256), 1)
    for group, side in enumerate((left_of, right_of)):
        rows_of = jnp.concatenate([side[...], rim_rows(left_rim, right_rim, group)], axis=0)
        total = dot(rows_of, middle[group])
        extra = total[512:528]
        total = total[0:512] + centre[:, group * 256 : (group + 1) * 256]
        total = total.reshape(8, 8, 8, 256)
        first = total[:, 0] + jnp.where(sub == 0, extra[0:8][:, None, :], 0.0)
        last = total[:, 7] + jnp.where(sub == 7, extra[8:16][:, None, :], 0.0)
        total = jnp.concatenate([first[:, None], total[:, 1:7], last[:, None]], axis=1)
        totals.append(total.reshape(512, 256))
    lane = iota((512, 128), 1)
    is_first = (lane & 31) < 8
    scales = []
    for half in range(2):
        s = jnp.where(is_first, jax.nn.sigmoid(totals[0][:, half * 128 : half * 128 + 128]), 0.0)
        s = s + pltpu.roll(s, 8, 1)
        scales.append(s + pltpu.roll(s, 16, 1))
    scale = jnp.concatenate(scales + scales, axis=1)
    total = jnp.concatenate(totals, axis=1)
    own = jnp.concatenate(own_lines(ends, inner), axis=0).astype(F32)
    bottleneck = (own + total * scale).astype(BF16)
    for group in range(2):
        span = slice(group * 256, (group + 1) * 256)
        for part in range(2):
            lows[part, span, :] = dot_nt(
                mixes[group], bottleneck[part * 256 : (part + 1) * 256, span]
            )
    size = 512 // chunks
    per = 8 // chunks
    copies = []
    for n in range(chunks):
        for line in range(8):
            scale = None
            for group in range(2):
                at = group * 256 + n * per * 32
                index = (iota((per * 32, 128), 1) >> 1) + (line % 2) * 64
                column = ((line % 4) // 2) * 128
                low = lows[line // 4, at : at + per * 32, column : column + 128]
                low = jnp.take_along_axis(low, index, axis=1)
                y = halves[line, at : at + per * 32, :] + jnp.concatenate([low, low], axis=1)
                if group == 0:
                    scale = gates(y)
                d = gated(y, scale)
                for half in range(2):
                    for c in range(per):
                        for b in range(4):
                            start = row_start(n * per + c, COMPONENTS[group][b]) + 2 * line + half
                            at = c * 32 + b * 8
                            wide[pl.ds(start, 8, stride=PITCH), :] = d[
                                at : at + 8, half * 128 : half * 128 + 128
                            ]
        for m in range(size // 8):
            at = (n * size // 8 + m) * PITCH
            piece = wide[at : at + 128, :].astype(BF16)
            out[n * size + m * 8 : n * size + m * 8 + 8] = piece.reshape(8, 16, 128)
        span = pl.ds(n * size, size)
        copies.append(pltpu.make_async_copy(out.at[span], decoded.at[span], sems.at[n]))
        copies[-1].start(priority=n % 2)
    for copy in copies:
        copy.wait()


VMEM = pl.BlockSpec(memory_space=pltpu.VMEM)
HBM = pl.BlockSpec(memory_space=pltpu.HBM)
UNROLL = True
PITCH = 136


def call(kernel, name, ins, outs, shapes, scratch, mebibytes, aliases={}):
    return pl.pallas_call(
        kernel,
        out_shape=shapes,
        in_specs=ins,
        out_specs=outs,
        scratch_shapes=scratch,
        compiler_params=pltpu.CompilerParams(vmem_limit_bytes=mebibytes * 1024 * 1024),
        name=name,
        input_output_aliases=aliases,
    )


def arr(*dims, dtype=BF16):
    return jax.ShapeDtypeStruct(dims, dtype)


def per_device(fields, enc_mix, k_cycle, centre_mix, dec_mix):
    rows, cols = lax.axis_size("row"), lax.axis_size("col")
    k_local = k_cycle.T
    shape = k_local.shape

    def shift(array, step):
        return lax.ppermute(array, "row", [(i, (i + step) % rows) for i in range(rows)])

    turns = jnp.asarray(np.stack([turn_table(t) for t in (1, 2, 3)]), BF16)
    chunks = 4
    wide, edges, ends, pay_down, pay_up, pay_own, mixes = call(
        functools.partial(edge_kernel, chunks=chunks),
        "edges",
        [HBM] * 4,
        (VMEM,) * 7,
        (
            arr(64 * PITCH, 128, dtype=F32), arr(2, 512, 256), arr(2, 64, 512),
            arr(88, 512), arr(88, 512), arr(24, 512), arr(2, 256, 256),
        ),
        [
            pltpu.VMEM((512, 16, 128), BF16),
            pltpu.VMEM(enc_mix.shape, BF16),
            pltpu.VMEM(shape, BF16),
            pltpu.VMEM(centre_mix.shape, BF16),
            pltpu.SemaphoreType.DMA((chunks,)),
            pltpu.SemaphoreType.DMA((3,)),
        ],
        24,
    )(*[pltpu.with_memory_space_constraint(x, pltpu.HBM) for x in (fields, enc_mix, k_local, centre_mix)])

    above, below = shift(pay_down, 1), shift(pay_up, -1)
    others = [shift(pay_own, step) for step in range(2, rows - 1)]
    inner, halves, out_mixes, order = call(
        inner_kernel,
        "inner",
        [VMEM] * 4,
        (VMEM,) * 4,
        (arr(6, 64, 512), arr(8, 512, 256, dtype=F32), arr(2, 256, 256), arr(512, 512)),
        [],
        24,
    )(wide, edges, mixes, dec_mix)
    near_out, far_out, block, half = call(
        functools.partial(rims_kernel, rows=rows, shape=shape),
        "rims",
        [VMEM] * (3 + rows),
        (VMEM,) * 4,
        (arr(shape[0] + 48, 512), arr(shape[0] + 16, 512), arr(shape[0], 512), arr(32, 512)),
        [pltpu.VMEM((rows,) + shape, BF16), pltpu.VMEM((64, 256), F32)],
        16,
    )(ends, inner, pay_own, above, below, *others, order)

    def mates(array):
        return lax.ppermute(array, "col", [(i, i ^ 1) for i in range(cols)])

    near = mates(near_out)
    far = lax.ppermute(
        far_out, "col", [(i, (i - 1 if i % 2 == 0 else i + 1) % cols) for i in range(cols)]
    )
    near_pairs = [
        lax.ppermute(
            block, "col", [((i + (even, odd)[i % 2]) % cols, i) for i in range(cols)]
        )
        for even, odd in pair_steps(cols)
    ]
    left_of, right_of = call(
        functools.partial(taps_kernel, rows=rows),
        "taps",
        [VMEM] * 4,
        (VMEM,) * 2,
        (arr(512, 2048), arr(512, 2048)),
        [pltpu.VMEM((10, 80, 512), F32), pltpu.VMEM((3, 10, 64, 512), BF16)],
        24,
    )(ends, inner, above, below)
    centre = call(
        functools.partial(centre_kernel, rows_in=shape[0]),
        "centre",
        [VMEM] * 4,
        VMEM,
        arr(512, 512, dtype=F32),
        [],
        16,
    )(ends, inner, half, near)
    def relay(array):
        return mates(lax.optimization_barrier((array, left_of, right_of, centre))[0])

    relayed = [relay(array) for array in [far] + near_pairs]
    split = shape[0] == 64
    scratch = [
        pltpu.VMEM((2048, 128), F32),
        pltpu.VMEM((2, 512, 256), F32),
        pltpu.VMEM((64 * PITCH, 128), F32),
        pltpu.VMEM((512, 16, 128), BF16),
        pltpu.SemaphoreType.DMA((chunks,)),
    ]
    kernel = functools.partial(final_kernel, cols=cols, shape=shape, chunks=chunks, split=split)
    operands = [ends, inner, halves, out_mixes, left_of, right_of, centre, near, far]
    result = jax.ShapeDtypeStruct(fields.shape, BF16)
    if not split:
        operands += [block] + near_pairs + relayed + [turns]
        scratch = [pltpu.VMEM((512, 512), BF16), pltpu.VMEM((2, 2048, 256), BF16)] + scratch
        return call(kernel, "final", [VMEM] * len(operands), HBM, result, scratch, 40)(*operands)
    middle = call(
        functools.partial(early_kernel, cols=cols, rows_in=shape[0]),
        "early",
        [VMEM] * (4 + len(near_pairs)),
        VMEM,
        arr(2, 2048, 256),
        [pltpu.VMEM((2048, 128), F32)],
        24,
    )(block, near, far, *near_pairs, turns)
    operands += relayed + [turns, middle]
    return call(
        kernel, "final", [VMEM] * len(operands), (HBM, VMEM), (result, arr(2, 2048, 256)),
        scratch, 40, aliases={len(operands) - 1: 1},
    )(*operands)[0]


def solution(mesh):
    return jax.shard_map(
        per_device,
        mesh=mesh,
        in_specs=(P(None, "row", "col"), P(), P("row", "col"), P(None, "row", None), P()),
        out_specs=P(None, "row", "col"),
        check_vma=False,
    )
```

```python
import functools
import math

import jax
import jax.numpy as jnp
import numpy as np
from jax import lax
from jax.experimental import pallas as pl
from jax.experimental.pallas import tpu as pltpu
from jax.sharding import PartitionSpec as P

F32, BF16 = jnp.float32, jnp.bfloat16

COMPONENTS = ((0, 1, 4, 5), (2, 3, 6, 7))
TAPS = ((0, 1), (1, 1), (1, 0), (1, -1))


def turn_signs(turn):
    signs = np.zeros((8, 8), np.int64)
    signs[0, 0] = 1
    signs[1, 1] = (-1) ** turn
    for frequency in range(1, 4):
        angle = 2.0 * math.pi * frequency * turn / 8.0
        cosine, sine = np.cos(angle), np.sin(angle)
        block = np.array([[cosine, -sine], [sine, cosine]])
        block[np.abs(block) < 0.1] = 0.0
        first = 2 * frequency
        signs[first : first + 2, first : first + 2] = np.sign(block)
    return signs


def turn_table(turn):
    signs = turn_signs(turn)
    table = np.zeros((2, 256, 256), np.float32)
    for group in range(2):
        for b_from in range(4):
            for b_to in range(4):
                sign = signs[COMPONENTS[group][b_to], COMPONENTS[group][b_from]]
                if sign:
                    for c in range(8):
                        for m in range(8):
                            table[group, c * 32 + b_from * 8 + m, c * 32 + b_to * 8 + m] = sign
    return table


def iota(shape, dim):
    return lax.broadcasted_iota(jnp.int32, shape, dim)


def spread_table():
    r, s = iota((256, 256), 0), iota((256, 256), 1)
    target = ((r & 63) >> 3) * 32 + (r >> 6) * 8 + (r & 7)
    return jnp.where(s == target, 1.0, 0.0).astype(BF16)


def order_table():
    r, s = iota((512, 512), 0), iota((512, 512), 1)
    field, component = r >> 3, r & 7
    group, b = (component >> 1) & 1, (component & 1) + 2 * (component >> 2)
    target = group * 256 + (field >> 3) * 32 + b * 8 + (field & 7)
    return jnp.where(s == target, 1.0, 0.0).astype(BF16)


def pool_table():
    x, column = iota((64, 256), 1), iota((64, 256), 0)
    return jnp.where(((x & 127) >> 1) == column, 0.25, 0.0).astype(BF16)


def dot(a, b):
    return jnp.dot(a, b, preferred_element_type=F32)


def dot_nt(a, b):
    return lax.dot_general(a, b, (((1,), (1,)), ((), ())), preferred_element_type=F32)


def mix_matrix(piece, spread, group):
    parts = [spread[b * 64 : (b + 1) * 64] for b in range(4)]
    if group == 0:
        rows = [dot(piece(0), parts[0]), dot(piece(1), parts[1])]
        u, v = 4, 5
    else:
        rows = [
            dot(piece(2), parts[0]) - dot(piece(3), parts[1]),
            dot(piece(3), parts[0]) + dot(piece(2), parts[1]),
        ]
        u, v = 6, 7
    rows += [
        dot(piece(u), parts[2]) - dot(piece(v), parts[3]),
        dot(piece(v), parts[2]) + dot(piece(u), parts[3]),
    ]
    chunks = [rows[b][c * 8 : (c + 1) * 8] for c in range(8) for b in range(4)]
    return jnp.concatenate(chunks, axis=0).astype(BF16)


def row_start(c, component):
    return c * 8 * PITCH + component * 16


def gather_rows(wide, y, group):
    chunks = [
        wide[pl.ds(row_start(c, COMPONENTS[group][b]) + y, 8, stride=PITCH), :]
        for c in range(8)
        for b in range(4)
    ]
    return jnp.concatenate(chunks, axis=0)


def gates(values):
    trivial = values.reshape(-1, 4, 8, values.shape[1])[:, 0]
    return jax.nn.sigmoid(trivial)


def gated(values, scale):
    split = values.reshape(-1, 4, 8, values.shape[1])
    return (split * scale[:, None]).reshape(values.shape)


def encode_line(wide, line, mixes, pool_t):
    result = []
    scale = None
    for group in range(2):
        x = jnp.concatenate(
            [gather_rows(wide, 2 * line, group), gather_rows(wide, 2 * line + 1, group)], axis=1
        )
        y = dot(mixes[group], x.astype(BF16))
        if group == 0:
            scale = gates(y)
        result.append((x + gated(y, scale)).astype(BF16))
    mean = dot_nt(pool_t, jnp.concatenate(result, axis=0))
    return result, mean.astype(BF16)


def edge_kernel(
    fields_in, weights_in, k_in, centre_in,
    wide, encoded, pooled, pay_down, pay_up, pay_own, mixes_out,
    held, weights, k_local, centre, sems, small, *, chunks,
):
    starts = []
    for n, (source, target) in enumerate(
        ((weights_in, weights), (k_in, k_local), (centre_in, centre))
    ):
        starts.append(pltpu.make_async_copy(source, target, small.at[n]))
        starts[-1].start()
    size = 512 // chunks
    copies = []
    for n in range(chunks):
        span = pl.ds(n * size, size)
        copies.append(pltpu.make_async_copy(fields_in.at[span], held.at[span], sems.at[n]))
        copies[-1].start(priority=n % 2)
    table = spread_table()
    pool_t = pool_table()
    for start in starts:
        start.wait()
    mixes = [mix_matrix(lambda s: weights[s], table, group) for group in range(2)]
    for group in range(2):
        mixes_out[group] = mixes[group]
    rows_in, cols_in = k_local.shape
    own_rows = centre.shape[1]
    for j in range(rows_in // 16):
        pay_own[0:16, j * cols_in : (j + 1) * cols_in] = k_local[j * 16 : (j + 1) * 16, :]
    first = 4 * lax.rem(lax.axis_index("col"), 2)
    part = jnp.concatenate([centre[first + s].astype(F32) for s in range(4)], axis=1)
    for j in range(own_rows // 8):
        pay_own[16:24, j * 256 : (j + 1) * 256] = part[j * 8 : (j + 1) * 8].astype(BF16)
    for n in range(chunks):
        copies[n].wait()
        piece = held[n * size : (n + 1) * size].astype(F32)
        piece = piece.reshape(size * 16, 128)
        for m in range(size // 8):
            at = (n * size // 8 + m) * PITCH
            wide[at : at + 128, :] = piece[m * 128 : m * 128 + 128]
    for n, (target, line) in enumerate(((pay_up, 0), (pay_down, 7))):
        result, mean = encode_line(wide, line, mixes, pool_t)
        encoded[n, 0:256, :] = result[0]
        encoded[n, 256:512, :] = result[1]
        pooled[n] = mean
        target[0:64, :] = mean
        target[64:88, :] = pay_own[...]


def inner_kernel(wide, edges, mixes_in, weights, pooled, halves, mixes_out, order):
    order[...] = order_table()
    table = spread_table()
    pool_t = pool_table()
    mixes = [mixes_in[group] for group in range(2)]
    ends = [mix_matrix(lambda s: weights[s], table, group) for group in range(2)]
    for group in range(2):
        mixes_out[group] = ends[group]

    def step(n, carry):
        result, mean = encode_line(wide, n + 1, mixes, pool_t)
        pooled[n] = mean
        for group in range(2):
            halves[n + 1, group * 256 : (group + 1) * 256, :] = dot(ends[group], result[group])
        return carry

    lax.fori_loop(0, 6, step, 0, unroll=UNROLL)
    for n, line in enumerate((0, 7)):
        for group in range(2):
            span = slice(group * 256, (group + 1) * 256)
            halves[line, span, :] = dot(ends[group], edges[n, span, :])


def rims_kernel(*refs, rows, shape):
    rows_in, cols_in = shape
    ends, inner, own, above, below = refs[:5]
    others = refs[5 : 5 + rows - 3]
    order = refs[2 + rows]
    near, far, block, half, raw, parts = refs[3 + rows :]
    row, col = lax.axis_index("row"), lax.axis_index("col")

    own_rows = 64 // rows

    def put(source, start, index):
        for j in range(rows_in // 16):
            raw[index, j * 16 : (j + 1) * 16, :] = source[
                start : start + 16, j * cols_in : (j + 1) * cols_in
            ]
        part = source[start + 16 : start + 24, :].astype(F32)
        for j in range(own_rows // 8):
            place = pl.multiple_of(index * own_rows + j * 8, 8)
            parts[pl.ds(place, 8), :] = part[:, j * 256 : (j + 1) * 256]

    put(own, 0, row)
    put(above, 64, lax.rem(row + rows - 1, rows))
    put(below, 64, lax.rem(row + 1, rows))
    for n, other in enumerate(others):
        put(other, 0, lax.rem(row + rows - 2 - n, rows))
    joined = jnp.concatenate([raw[r] for r in range(rows)], axis=1)
    sorted_block = dot(joined, order[...]).astype(BF16)
    block[...] = sorted_block
    lines = all_lines(ends, inner, above, below, row, rows)
    blank = jnp.zeros((6, 512), F32)
    left = jnp.concatenate([line[0:1] for line in lines] + [blank], axis=0)
    right = jnp.concatenate([line[63:64] for line in lines] + [blank], axis=0)
    even = lax.rem(col, 2) == 0
    near[0:rows_in, :] = sorted_block
    far[0:rows_in, :] = sorted_block
    half[...] = jnp.concatenate([parts[0:32, :], parts[32:64, :]], axis=1).astype(BF16)
    near[rows_in + 16 : rows_in + 48, :] = half[...]
    near[rows_in : rows_in + 16, :] = jnp.where(even, right, left).astype(BF16)
    far[rows_in : rows_in + 16, :] = jnp.where(even, left, right).astype(BF16)


def own_lines(ends, inner):
    return [ends[0]] + [inner[line] for line in range(6)] + [ends[1]]


def all_lines(ends, inner, above, below, row, rows):
    top = jnp.where(row > 0, above[0:64, :].astype(F32), 0.0)
    bottom = jnp.where(row < rows - 1, below[0:64, :].astype(F32), 0.0)
    return [top] + [line.astype(F32) for line in own_lines(ends, inner)] + [bottom]


def taps_kernel(*refs, rows):
    ends, inner, above, below, left_of, right_of, padded, shifted = refs
    row = lax.axis_index("row")
    zero = jnp.zeros((1, 512), F32)
    for line, values in enumerate(all_lines(ends, inner, above, below, row, rows)):
        padded[line, 8:72, :] = values
        padded[line, 7:8, :] = zero
        padded[line, 72:73, :] = zero
        shifted[1, line] = values.astype(BF16)
        shifted[0, line] = padded[line, 7:71, :].astype(BF16)
        shifted[2, line] = padded[line, 9:73, :].astype(BF16)
    for line in range(8):
        span = slice(line * 64, line * 64 + 64)
        for tap, (dy, dx) in enumerate(TAPS):
            ahead = shifted[1 + dx, line + 1 + dy]
            behind = shifted[1 - dx, line + 1 - dy]
            plus, minus = ahead + behind, ahead - behind
            base = tap * 512
            left_of[span, base : base + 256] = plus[:, :256]
            left_of[span, base + 256 : base + 512] = minus[:, 256:]
            right_of[span, base : base + 256] = minus[:, :256]
            right_of[span, base + 256 : base + 512] = plus[:, 256:]


def pair_steps(cols):
    steps_even = list(range(4, cols, 2))
    steps_odd = steps_even[:-1] + [2]
    return list(zip(steps_even, steps_odd))


def rim_rows(left_rim, right_rim, group):
    parts = []
    for dy, dx in TAPS:
        if dx == 0:
            parts += [jnp.zeros((16, 512), F32)]
            continue
        first = left_rim[1 - dx * dy : 9 - dx * dy]
        last = right_rim[1 + dx * dy : 9 + dx * dy]
        plus = jnp.concatenate([first, last], axis=0)
        minus = jnp.concatenate([first * float(-dx), last * float(dx)], axis=0)
        pair = (plus, minus) if group == 0 else (minus, plus)
        parts += [pair[0][:, :256], pair[1][:, 256:]]
    return jnp.concatenate(parts, axis=1).astype(BF16)


def turn_blocks(blocks, places, turns, turned, middle):
    root = math.sqrt(0.5)
    whole = jnp.concatenate(blocks, axis=0)
    count = whole.shape[0] // 64
    for tap in range(4):
        signs = turn_signs(tap)
        for group in range(2):
            side = whole[:, group * 256 : (group + 1) * 256]
            result = side.astype(F32) if tap == 0 else dot(side, turns[tap - 1, group])
            base = ((tap * 2 + group) % 2) * 1024
            turned[base : base + count * 64, :] = result[:, 0:128]
            turned[base + 512 : base + 512 + count * 64, :] = result[:, 128:256]
            for source in range(2):
                scale = 1.0
                if tap % 2:
                    scale = (1.0, root, 0.5)[group + source]
                comps = COMPONENTS[source]
                for n in range(count):
                    read = {
                        comp: jnp.concatenate(
                            [
                                turned[pl.ds(base + half * 512 + n * 64 + comp, 8, stride=8), :]
                                for half in range(2)
                            ],
                            axis=1,
                        )
                        for comp in comps
                    }
                    parts = []
                    for comp in comps:
                        total = None
                        for other in comps:
                            sign = int(signs[comp, other])
                            if sign == 0:
                                continue
                            if total is None:
                                total = read[other] if sign > 0 else -read[other]
                            else:
                                total = total + read[other] if sign > 0 else total - read[other]
                        parts.append(total if scale == 1.0 else total * scale)
                    start = pl.multiple_of(tap * 512 + source * 256 + places[n] * 32, 32)
                    middle[group, pl.ds(start, 32), :] = jnp.concatenate(parts, axis=0).astype(BF16)


def away(index, step_even, step_odd, cols):
    index = index + jnp.where(lax.rem(index, 2) == 0, step_even, step_odd)
    return lax.rem(index + 2 * cols, cols)


def block_places(col, cols):
    even = lax.rem(col, 2) == 0
    mate = jnp.where(even, col + 1, col - 1)
    steps = [(-1, 1)] + pair_steps(cols)
    first = [col, mate] + [away(col, a, b, cols) for a, b in steps]
    return first, [away(mate, a, b, cols) for a, b in steps]


def centre_kernel(ends, inner, half, near, centre, *, rows_in):
    even = lax.rem(lax.axis_index("col"), 2) == 0
    one = half[...].astype(F32)
    two = near[rows_in + 16 : rows_in + 48, :].astype(F32)
    halves = [
        jnp.where(even, one, two).astype(BF16),
        jnp.where(even, two, one).astype(BF16),
    ]

    def piece(s):
        at = (s % 4) * 64
        source = halves[s // 4]
        return jnp.concatenate(
            [source[:, at : at + 64], source[:, 256 + at : 320 + at]], axis=0
        )

    table = spread_table()
    whole = jnp.concatenate(own_lines(ends, inner), axis=0)
    for group in range(2):
        span = slice(group * 256, (group + 1) * 256)
        centre[:, span] = dot_nt(whole[:, span], mix_matrix(piece, table, group))


def early_kernel(*refs, cols, rows_in):
    blocks = refs[: 2 + cols // 2]
    turns, middle, turned = refs[2 + cols // 2 :]
    first, second = block_places(lax.axis_index("col"), cols)
    places = first + second[:1]
    turn_blocks([block[0:rows_in, :] for block in blocks], places, turns, turned, middle)


def final_kernel(*refs, cols, shape, chunks, split):
    rows_in, _ = shape
    relays = cols // 2 - 1
    ends, inner, halves, mixes, left_of, right_of, centre = refs[:7]
    near, far = refs[7:9]
    refs = refs[9:]
    col = lax.axis_index("col")
    even = lax.rem(col, 2) == 0
    first, second = block_places(col, cols)
    if split:
        relayed, turns = refs[:relays], refs[relays]
        decoded, middle, turned, lows, wide, out, sems = refs[relays + 2 :]
        late = [block[0:rows_in, :] for block in relayed[1:]]
        places = second[1:]
    else:
        held, relayed, turns = refs[: relays], refs[relays : 2 * relays], refs[2 * relays]
        decoded, kt, middle, turned, lows, wide, out, sems = refs[2 * relays + 1 :]
        for block, index in zip((held[0], near, far) + held[1:] + relayed, first + second):
            start = pl.multiple_of(index * rows_in, rows_in)
            kt[pl.ds(start, rows_in), :] = block[0:rows_in, :]
        late = [kt[...]]
        places = list(range(8))

    pending = list(late)
    turn_blocks(pending, places, turns, turned, middle)

    near_rim = near[rows_in : rows_in + 16, :].astype(F32)
    far_rim = far[rows_in : rows_in + 16, :].astype(F32)
    left_rim = jnp.where(even, far_rim, near_rim)
    right_rim = jnp.where(even, near_rim, far_rim)
    totals = []
    sub = iota((8, 8, 256), 1)
    for group, side in enumerate((left_of, right_of)):
        rows_of = jnp.concatenate([side[...], rim_rows(left_rim, right_rim, group)], axis=0)
        total = dot(rows_of, middle[group])
        extra = total[512:528]
        total = total[0:512] + centre[:, group * 256 : (group + 1) * 256]
        total = total.reshape(8, 8, 8, 256)
        first = total[:, 0] + jnp.where(sub == 0, extra[0:8][:, None, :], 0.0)
        last = total[:, 7] + jnp.where(sub == 7, extra[8:16][:, None, :], 0.0)
        total = jnp.concatenate([first[:, None], total[:, 1:7], last[:, None]], axis=1)
        totals.append(total.reshape(512, 256))
    lane = iota((512, 128), 1)
    is_first = (lane & 31) < 8
    scales = []
    for half in range(2):
        s = jnp.where(is_first, jax.nn.sigmoid(totals[0][:, half * 128 : half * 128 + 128]), 0.0)
        s = s + pltpu.roll(s, 8, 1)
        scales.append(s + pltpu.roll(s, 16, 1))
    scale = jnp.concatenate(scales + scales, axis=1)
    total = jnp.concatenate(totals, axis=1)
    own = jnp.concatenate(own_lines(ends, inner), axis=0).astype(F32)
    bottleneck = (own + total * scale).astype(BF16)
    for group in range(2):
        span = slice(group * 256, (group + 1) * 256)
        for part in range(2):
            lows[part, span, :] = dot_nt(
                mixes[group], bottleneck[part * 256 : (part + 1) * 256, span]
            )
    size = 512 // chunks
    per = 8 // chunks
    copies = []
    for n in range(chunks):
        for line in range(8):
            scale = None
            for group in range(2):
                at = group * 256 + n * per * 32
                index = (iota((per * 32, 128), 1) >> 1) + (line % 2) * 64
                column = ((line % 4) // 2) * 128
                low = lows[line // 4, at : at + per * 32, column : column + 128]
                low = jnp.take_along_axis(low, index, axis=1)
                y = halves[line, at : at + per * 32, :] + jnp.concatenate([low, low], axis=1)
                if group == 0:
                    scale = gates(y)
                d = gated(y, scale)
                for half in range(2):
                    for c in range(per):
                        for b in range(4):
                            start = row_start(n * per + c, COMPONENTS[group][b]) + 2 * line + half
                            at = c * 32 + b * 8
                            wide[pl.ds(start, 8, stride=PITCH), :] = d[
                                at : at + 8, half * 128 : half * 128 + 128
                            ]
        for m in range(size // 8):
            at = (n * size // 8 + m) * PITCH
            piece = wide[at : at + 128, :].astype(BF16)
            out[n * size + m * 8 : n * size + m * 8 + 8] = piece.reshape(8, 16, 128)
        span = pl.ds(n * size, size)
        copies.append(pltpu.make_async_copy(out.at[span], decoded.at[span], sems.at[n]))
        copies[-1].start(priority=n % 2)
    for copy in copies:
        copy.wait()


VMEM = pl.BlockSpec(memory_space=pltpu.VMEM)
HBM = pl.BlockSpec(memory_space=pltpu.HBM)
UNROLL = True
PITCH = 136


def call(kernel, name, ins, outs, shapes, scratch, mebibytes, aliases={}):
    return pl.pallas_call(
        kernel,
        out_shape=shapes,
        in_specs=ins,
        out_specs=outs,
        scratch_shapes=scratch,
        compiler_params=pltpu.CompilerParams(vmem_limit_bytes=mebibytes * 1024 * 1024),
        name=name,
        input_output_aliases=aliases,
    )


def arr(*dims, dtype=BF16):
    return jax.ShapeDtypeStruct(dims, dtype)


def per_device(fields, enc_mix, k_cycle, centre_mix, dec_mix):
    rows, cols = lax.axis_size("row"), lax.axis_size("col")
    k_local = k_cycle.T
    shape = k_local.shape

    def shift(array, step):
        return lax.ppermute(array, "row", [(i, (i + step) % rows) for i in range(rows)])

    turns = jnp.asarray(np.stack([turn_table(t) for t in (1, 2, 3)]), BF16)
    chunks = 4
    wide, edges, ends, pay_down, pay_up, pay_own, mixes = call(
        functools.partial(edge_kernel, chunks=chunks),
        "edges",
        [HBM] * 4,
        (VMEM,) * 7,
        (
            arr(64 * PITCH, 128, dtype=F32), arr(2, 512, 256), arr(2, 64, 512),
            arr(88, 512), arr(88, 512), arr(24, 512), arr(2, 256, 256),
        ),
        [
            pltpu.VMEM((512, 16, 128), BF16),
            pltpu.VMEM(enc_mix.shape, BF16),
            pltpu.VMEM(shape, BF16),
            pltpu.VMEM(centre_mix.shape, BF16),
            pltpu.SemaphoreType.DMA((chunks,)),
            pltpu.SemaphoreType.DMA((3,)),
        ],
        24,
    )(*[pltpu.with_memory_space_constraint(x, pltpu.HBM) for x in (fields, enc_mix, k_local, centre_mix)])

    above, below = shift(pay_down, 1), shift(pay_up, -1)
    others = [shift(pay_own, step) for step in range(2, rows - 1)]
    inner, halves, out_mixes, order = call(
        inner_kernel,
        "inner",
        [VMEM] * 4,
        (VMEM,) * 4,
        (arr(6, 64, 512), arr(8, 512, 256, dtype=F32), arr(2, 256, 256), arr(512, 512)),
        [],
        24,
    )(wide, edges, mixes, dec_mix)
    near_out, far_out, block, half = call(
        functools.partial(rims_kernel, rows=rows, shape=shape),
        "rims",
        [VMEM] * (3 + rows),
        (VMEM,) * 4,
        (arr(shape[0] + 48, 512), arr(shape[0] + 16, 512), arr(shape[0], 512), arr(32, 512)),
        [pltpu.VMEM((rows,) + shape, BF16), pltpu.VMEM((64, 256), F32)],
        16,
    )(ends, inner, pay_own, above, below, *others, order)

    def mates(array):
        return lax.ppermute(array, "col", [(i, i ^ 1) for i in range(cols)])

    near = mates(near_out)
    far = lax.ppermute(
        far_out, "col", [(i, (i - 1 if i % 2 == 0 else i + 1) % cols) for i in range(cols)]
    )
    near_pairs = [
        lax.ppermute(
            block, "col", [((i + (even, odd)[i % 2]) % cols, i) for i in range(cols)]
        )
        for even, odd in pair_steps(cols)
    ]
    left_of, right_of = call(
        functools.partial(taps_kernel, rows=rows),
        "taps",
        [VMEM] * 4,
        (VMEM,) * 2,
        (arr(512, 2048), arr(512, 2048)),
        [pltpu.VMEM((10, 80, 512), F32), pltpu.VMEM((3, 10, 64, 512), BF16)],
        24,
    )(ends, inner, above, below)
    centre = call(
        functools.partial(centre_kernel, rows_in=shape[0]),
        "centre",
        [VMEM] * 4,
        VMEM,
        arr(512, 512, dtype=F32),
        [],
        16,
    )(ends, inner, half, near)
    def relay(array):
        return mates(lax.optimization_barrier((array, left_of, right_of, centre))[0])

    relayed = [relay(array) for array in [far] + near_pairs]
    split = shape[0] == 64
    scratch = [
        pltpu.VMEM((2048, 128), F32),
        pltpu.VMEM((2, 512, 256), F32),
        pltpu.VMEM((64 * PITCH, 128), F32),
        pltpu.VMEM((512, 16, 128), BF16),
        pltpu.SemaphoreType.DMA((chunks,)),
    ]
    kernel = functools.partial(final_kernel, cols=cols, shape=shape, chunks=chunks, split=split)
    operands = [ends, inner, halves, out_mixes, left_of, right_of, centre, near, far]
    result = jax.ShapeDtypeStruct(fields.shape, BF16)
    if not split:
        operands += [block] + near_pairs + relayed + [turns]
        scratch = [pltpu.VMEM((512, 512), BF16), pltpu.VMEM((2, 2048, 256), BF16)] + scratch
        return call(kernel, "final", [VMEM] * len(operands), HBM, result, scratch, 40)(*operands)
    middle = call(
        functools.partial(early_kernel, cols=cols, rows_in=shape[0]),
        "early",
        [VMEM] * (5 + len(near_pairs)),
        VMEM,
        arr(2, 2048, 256),
        [pltpu.VMEM((2048, 128), F32)],
        24,
    )(block, near, far, *near_pairs, relayed[0], turns)
    operands += relayed + [turns, middle]
    return call(
        kernel, "final", [VMEM] * len(operands), (HBM, VMEM), (result, arr(2, 2048, 256)),
        scratch, 40, aliases={len(operands) - 1: 1},
    )(*operands)[0]


def solution(mesh):
    return jax.shard_map(
        per_device,
        mesh=mesh,
        in_specs=(P(None, "row", "col"), P(), P("row", "col"), P(None, "row", None), P()),
        out_specs=P(None, "row", "col"),
        check_vma=False,
    )
```
